256 devices in a mesh: chan: 16 (over z, core), rad: 16 (over y, x).
Axes of the slice: x: 4, y: 4, z: 8, core: 2. Of those that a mesh axis runs over, the one named last changes fastest.
Arguments:
- state: float32 [2048, 2, 16, 1536], P('chan', None, None, 'rad'), may hold values from -200 to 200
- coupling: float32 [64, 16, 4, 32, 32], P('chan'), may hold values from -1.1 to 1.1
- fetch_group: int32 [16, 16], replicated, may hold values from 0 to 3
- live_slots: int32 [64], P('chan'), may hold values from 1 to 16, as said below
- radius_one: float32 [16], replicated, may hold values from 1 to 6
- radius_two: float32 [1536], P('rad'), may hold values from 1 to 6
- kinetic_diag: float32 [12, 128, 128], replicated, may hold values from -2 to 5
- kinetic_link: float32 [11, 128, 128], replicated, may hold values from -0.5 to 0.5
Outputs:
- orthogonal: float32 [2048, 2, 16, 1536], P(('chan', 'rad'))
- arnoldi_coeffs: float32 [3], replicated
The draws below stay inside these ranges and needn't reach their ends.
Inputs may be any that keep to these rules, and one draw needn't show every extreme that they name: `live_slots`: every draw has a block with all 16 slots live.
All inputs are finite; a program needn't handle non-finite values.
Results may differ from the reference program's by a relative error of at most 0.0003.
Values sent between devices are 32-bit elements; how exact they have to be, the bound alone decides.
A program may use at most 128 MiB of HBM per device.

```python
import math
import jax
import jax.numpy as jnp
from jax import lax

C = 2048
GS = 32
R = 1536
P_SIZE = 128
LAM = 4
B = 16
NG = 64
GPD = 4
SLOTS = 16
NE = 12


def draw_state(key, part):
    first, second, third = jax.random.split(key, 3)
    chan_pos = jnp.arange(C, dtype=jnp.float32) / C
    rad_pos = jnp.arange(R, dtype=jnp.float32) / R
    chan_scale = jnp.exp(math.log(10.0) * (jax.random.uniform(second, (C,), jnp.float32) - 0.5)) * (1.0 + 0.8 * chan_pos)
    rad_scale = jnp.exp(math.log(10.0) * (jax.random.uniform(third, (R,), jnp.float32) - 0.5)) * (1.0 + 0.8 * rad_pos)
    phase = math.pi * chan_pos
    common = jnp.stack([jnp.cos(phase), jnp.sin(phase)], axis=1)[:, :, None, None]
    base = jax.random.truncated_normal(first, -5.0, 5.0, (C, 2, B, R), jnp.float32) + 0.8 * common
    return base * chan_scale[:, None, None, None] * rad_scale[None, None, None, :]


def draw_coupling(key, part):
    spread = (GS * LAM) ** (-0.5)
    noise = jax.random.truncated_normal(key, -4.0, 4.0, (NG, SLOTS, LAM, GS, GS), jnp.float32) * spread
    offset = 0.025
    return noise + offset


def draw_live_slots(key, part):
    first, second, third, fourth = jax.random.split(key, 4)
    light = jax.random.randint(first, (NG,), 1, max(2, SLOTS // 4) + 1)
    heavy = jax.random.randint(second, (NG,), SLOTS // 2, SLOTS + 1)
    ranking = jax.random.permutation(third, SLOTS)
    owner = jnp.arange(NG) // GPD
    is_heavy = jnp.take(ranking, owner) < max(1, SLOTS // 4)
    values = jnp.where(is_heavy, heavy, light)
    chosen = jax.random.randint(fourth, (), 0, NG)
    values = jnp.where(jnp.arange(NG) == chosen, SLOTS, values)
    return values.astype(jnp.int32)


def draw_kinetic_diag(key, part):
    first, second = jax.random.split(key)
    spread = jax.random.truncated_normal(first, -4.0, 4.0, (NE, P_SIZE, P_SIZE), jnp.float32) * P_SIZE ** (-0.5)
    diagonal = jax.random.uniform(second, (NE, P_SIZE), jnp.float32, 1.0, 3.0)
    return spread + diagonal[:, :, None] * jnp.eye(P_SIZE, dtype=jnp.float32)[None]


def touch_ends(drawn, rng, smallest, top_value):
    longest = drawn.shape.index(max(drawn.shape))
    spots = []
    for shift in (0, 1):
        where = [jax.random.randint(jax.random.fold_in(rng, axis), (), 0, length) for axis, length in enumerate(drawn.shape)]
        where[longest] = (where[longest] + shift) % drawn.shape[longest]
        spots.append(tuple(where))
    return drawn.at[spots[0]].set(smallest).at[spots[1]].set(top_value)


def block_scale(stream_key, dims, pieces, low, top_value):
    loudness = 1.0
    for position, shards_of in pieces:
        steps = jax.random.uniform(jax.random.fold_in(jax.random.fold_in(stream_key, 6), position), (shards_of,), jnp.float32, low / len(pieces), top_value / len(pieces))
        loudness = loudness * jnp.repeat(jnp.exp(steps), dims[position] // shards_of).reshape((-1,) + (1,) * (len(dims) - 1 - position))
    return loudness


def gaussian(key, extent, scale, reach, kind=jnp.bfloat16):
    return jnp.clip(scale * jax.random.normal(key, extent, jnp.float32), -reach, reach).astype(kind)


def setup_inputs(seed: int = 0) -> dict:
    splits = jax.random.split(jax.random.key(seed), 9)
    state = draw_state(jax.random.fold_in(splits[8], 71), 0)
    coupling = draw_coupling(jax.random.fold_in(splits[8], 71), 0)
    fetch_group = touch_ends(jax.random.randint(splits[2], (SLOTS, SLOTS), 0, GPD), jax.random.fold_in(splits[2], 1), 0, GPD - 1).astype(jnp.int32)
    live_slots = draw_live_slots(jax.random.fold_in(splits[8], 71), 0)
    radius_one = jnp.clip(jax.random.uniform(splits[4], (B,), jnp.float32, 1.0, 6.0), 1.0, 6.0)
    radius_two = jnp.clip(1.0 + 5.0 * jax.random.uniform(splits[5], (R,), jnp.float32) ** block_scale(splits[5], (R,), ((0, 16),), -0.2, 0.2), 1.0, 6.0)
    kinetic_diag = draw_kinetic_diag(jax.random.fold_in(splits[8], 71), 0)
    kinetic_link = gaussian(splits[7], (NE - 1, P_SIZE, P_SIZE), P_SIZE ** -0.5, 0.5, jnp.float32)
    return dict(state=state, coupling=coupling, fetch_group=fetch_group, live_slots=live_slots, radius_one=radius_one, radius_two=radius_two, kinetic_diag=kinetic_diag, kinetic_link=kinetic_link)


def radial_kernel(radius_one, radius_two, orders):
    nearer = jnp.minimum(radius_one[:, None], radius_two[None, :])
    farther = jnp.maximum(radius_one[:, None], radius_two[None, :])
    powers = jnp.arange(orders).astype(radius_one.dtype)[:, None, None]
    return nearer[None] ** powers / farther[None] ** (powers + 1.0)

def kinetic(field, kinetic_diag, kinetic_link):
    elements = kinetic_diag.shape[0]
    points = kinetic_diag.shape[1]
    rows = field.reshape(-1, elements, points)
    result = jnp.einsum('rep,eqp->req', rows, kinetic_diag, precision=lax.Precision.HIGHEST)
    lower = jnp.einsum('rep,eqp->req', rows[:, :-1], kinetic_link, precision=lax.Precision.HIGHEST)
    upper = jnp.einsum('rep,epq->req', rows[:, 1:], kinetic_link, precision=lax.Precision.HIGHEST)
    result = result + jnp.pad(lower, ((0, 0), (1, 0), (0, 0))) + jnp.pad(upper, ((0, 0), (0, 1), (0, 0)))
    return result.reshape(field.shape)

def reference(state, coupling, fetch_group, live_slots, radius_one, radius_two, kinetic_diag, kinetic_link):
    kernel = radial_kernel(radius_one, radius_two, LAM)
    grouped = state.reshape(NG, GS, 2, B, R)

    def one_device(device):
        slots = jnp.arange(SLOTS).astype(jnp.int32)
        sources = ((device + slots) % SLOTS).astype(jnp.int32)
        picked = (sources * GPD + jnp.take(fetch_group[device], sources)).astype(jnp.int32)
        slabs = jnp.take(grouped, picked, axis=0)
        weights = lax.dynamic_slice_in_dim(coupling, (device * GPD).astype(jnp.int32), GPD, 0)
        lives = lax.dynamic_slice_in_dim(live_slots, (device * GPD).astype(jnp.int32), GPD, 0)
        active = (slots[None, :] < lives[:, None]).astype(state.dtype)
        weights = weights * active[:, :, None, None, None]
        products = jnp.einsum('gkaij,kjpbr->agipbr', weights, slabs, precision=lax.Precision.HIGHEST)
        return lax.optimization_barrier(jnp.sum(products * kernel[:, None, None, None, :, :], axis=0))
    coupled = lax.map(one_device, jnp.arange(SLOTS).astype(jnp.int32)).reshape(C, 2, B, R)
    applied = kinetic(state, kinetic_diag, kinetic_link) + coupled
    wave_re = applied[:, 1]
    wave_im = -applied[:, 0]
    state_re = state[:, 0]
    state_im = state[:, 1]
    cross_re = jnp.sum(state_re * wave_re + state_im * wave_im)
    cross_im = jnp.sum(state_re * wave_im - state_im * wave_re)
    self_sq = jnp.sum(state * state)
    proj_re = cross_re / self_sq
    proj_im = cross_im / self_sq
    orth_re = wave_re - (proj_re * state_re - proj_im * state_im)
    orth_im = wave_im - (proj_re * state_im + proj_im * state_re)
    square_mean = jnp.sum(orth_re * orth_re + orth_im * orth_im) / (2.0 * C * B * R)
    rms = jnp.sqrt(square_mean + 1e-06)
    orthogonal = jnp.stack([orth_re, orth_im], axis=1)
    return (orthogonal, jnp.stack([proj_re, proj_im, rms]))
```

```python
import functools

import jax
import jax.numpy as jnp
from jax import lax
from jax.experimental import pallas as pl
from jax.experimental.pallas import tpu as pltpu
from jax.sharding import PartitionSpec as P

MESH = pl.DeviceIdType.MESH
F32 = jnp.float32
BF16 = jnp.bfloat16

C = 2048
R = 1536
B = 16
DEV = 16
Q = 4
CELLS = 768
GS = 32
T = 12
GROUPS = 1 + T // 2
LANES = 128
PTS = 96


def split(x):
    high = x.astype(BF16)
    return high, (x - high.astype(F32)).astype(BF16)


def pack4(a, b, c, d):
    return (
        jnp.concatenate([a, d[:, 0:32]], axis=1),
        jnp.concatenate([b, d[:, 32:64]], axis=1),
        jnp.concatenate([c, d[:, 64:96]], axis=1),
    )


def unpack4(t0, t1, t2):
    last = jnp.concatenate([t0[:, 96:128], t1[:, 96:128], t2[:, 96:128]], axis=1)
    return t0[:, 0:96], t1[:, 0:96], t2[:, 0:96], last


def kernel(
    state_ref,
    coup_ref,
    fetch_ref,
    live_ref,
    r1_ref,
    r2_ref,
    diag_ref,
    link_ref,
    out_ref,
    coef_ref,
    xp,
    sibx,
    pool,
    stage,
    wh,
    wl,
    kern,
    acc,
    cpl,
    srecv,
    crecv,
    snat,
    app,
    rows_of,
    part,
    gath,
    ring_send,
    ring_recv,
    sib_send,
    sib_recv,
    sx_send,
    sx_recv,
    st_send,
    st_recv,
    cp_send,
    cp_recv,
    sc_send,
    sc_recv,
):
    me = lax.axis_index("chan")
    rad = lax.axis_index("rad")
    core = lax.rem(me, 2)
    sib = me + 1 - 2 * core
    up = (lax.rem(me + 2, DEV), rad)
    down = (lax.rem(me + DEV - 2, DEV), rad)
    sibling = (sib, rad)

    def chan_peer(k):
        return (lax.rem(me + k, DEV), rad)

    def rad_peer(k):
        return (me, lax.rem(rad + k, DEV))

    barrier = pltpu.get_barrier_semaphore()
    for k in range(1, DEV):
        pl.semaphore_signal(barrier, inc=1, device_id=chan_peer(k), device_id_type=MESH)
        pl.semaphore_signal(barrier, inc=1, device_id=rad_peer(k), device_id_type=MESH)

    for q in range(Q):
        for plane in range(2):
            rows = [
                state_ref[pl.ds(plane * B + 4 * q + i, 128, stride=2 * B), :]
                for i in range(4)
            ]
            for i, tile in enumerate(pack4(*rows)):
                at = (plane * 3 + i) * LANES
                xp[q, :, at : at + LANES] = tile

    pl.semaphore_wait(barrier, 2 * (DEV - 1))

    def slot(t, side, way):
        return (t * 4 + side * 2 + way) * GS

    def ring_copy(q, t, way, src):
        return pltpu.make_async_remote_copy(
            src_ref=src,
            dst_ref=pool.at[q, pl.ds(slot(t, 0, way), GS), :],
            send_sem=ring_send.at[way, q, t],
            recv_sem=ring_recv.at[way, q, t],
            device_id=(up, down)[way],
            device_id_type=MESH,
        )

    def ring_src(q, t, way):
        if t < 4:
            return xp.at[q, pl.ds(GS * t, GS), :]
        if t < 8:
            return pool.at[q, pl.ds(slot(t - 4, 0, way), GS), :]
        if t < 11:
            return stage.at[q, way * 3 + t - 8]
        return pool.at[q, pl.ds(slot(10, 0, way), GS), :]

    def fetched(dest, source):
        return fetch_ref[dest, source]

    def wrap(x):
        return lax.rem(x + 2 * DEV, DEV)

    picks = []
    for way in range(2):
        sign = 1 if way == 0 else -1
        source = wrap(me - 4 * sign)
        near = wrap(me - core + 2 * sign)
        far = wrap(me - core + 4 * sign)
        far_core = core if way == 0 else 1 - core
        picks.append(
            [
                fetched(near, source),
                fetched(near + 1, source),
                fetched(far + far_core, source),
            ]
        )

    def ring_start(q, t):
        for way in range(2):
            if 8 <= t < 11:
                pick = picks[way][t - 8]
                chosen = pool[q, pl.ds(slot(4, 0, way), GS), :]
                for h in range(1, 4):
                    chosen = jnp.where(
                        pick == h, pool[q, pl.ds(slot(4 + h, 0, way), GS), :], chosen
                    )
                stage[q, way * 3 + t - 8] = chosen
            ring_copy(q, t, way, ring_src(q, t, way)).start()

    def sib_copy(q, t):
        return pltpu.make_async_remote_copy(
            src_ref=pool.at[q, pl.ds(slot(t, 0, 0), 2 * GS), :],
            dst_ref=pool.at[q, pl.ds(slot(t, 1, 0), 2 * GS), :],
            send_sem=sib_send.at[q, t],
            recv_sem=sib_recv.at[q, t],
            device_id=sibling,
            device_id_type=MESH,
        )

    def arrived(q, t):
        for way in range(2):
            ring_copy(q, t, way, ring_src(q, t, way)).wait_recv()
        sib_copy(q, t).start()

    def sib_arrived(q, t):
        sib_copy(q, t).wait_recv()

    sibx_copy = pltpu.make_async_remote_copy(
        src_ref=xp,
        dst_ref=sibx,
        send_sem=sx_send.at[0],
        recv_sem=sx_recv.at[0],
        device_id=sibling,
        device_id_type=MESH,
    )

    def state_copy(k):
        return pltpu.make_async_remote_copy(
            src_ref=xp.at[:, pl.ds(8 * lax.rem(rad + k, DEV), 8), :],
            dst_ref=srecv.at[rad],
            send_sem=st_send.at[k],
            recv_sem=st_recv.at[k],
            device_id=rad_peer(k),
            device_id_type=MESH,
        )

    def coupled_copy(q, k):
        return pltpu.make_async_remote_copy(
            src_ref=cpl.at[q, pl.ds(8 * lax.rem(rad + k, DEV), 8), :],
            dst_ref=crecv.at[q, rad],
            send_sem=cp_send.at[q, k],
            recv_sem=cp_recv.at[q, k],
            device_id=rad_peer(k),
            device_id_type=MESH,
        )

    ring_start(0, 0)
    ring_start(0, 1)
    sibx_copy.start()
    for k in range(1, DEV):
        state_copy(k).start()
    ring_start(0, 2)
    ring_start(0, 3)
    srecv[rad] = xp[:, pl.ds(pl.multiple_of(8 * rad, 8), 8), :]

    row = jnp.broadcast_to(r2_ref[0:1, :], (8, PTS))
    tails = pack4(row, row, row, row)
    lane = lax.broadcasted_iota(jnp.int32, (8, LANES), 1)
    for q in range(Q):
        for i in range(3):
            one = jnp.where(lane < PTS, r1_ref[4 * q + i], r1_ref[4 * q + 3])
            nearer = jnp.minimum(one, tails[i])
            farther = jnp.maximum(one, tails[i])
            top = jnp.ones_like(nearer)
            bottom = farther
            for order in range(4):
                value = top / bottom
                for plane in range(2):
                    at = (plane * 3 + i) * LANES
                    kern[q, order, :, at : at + LANES] = value
                top = top * nearer
                bottom = bottom * farther

    def put_weight(group, place, k, take):
        for g in range(4):
            on = jnp.where(live_ref[g] > k, take, 0.0)
            for order in range(4):
                start = ((g * 16 + k) * 4 + order) * GS
                block = coup_ref[pl.ds(pl.multiple_of(start, GS), GS), :] * on
                high, low = split(block)
                rows = slice(order * 128 + g * GS, order * 128 + g * GS + GS)
                cols = slice(place * GS, place * GS + GS)
                wh[group, rows, cols] = high
                wl[group, rows, cols] = low

    def one_if(condition):
        return jnp.where(condition, 1.0, 0.0)

    def build(group):
        if group == 0:
            for h in range(4):
                put_weight(0, h, 0, one_if(fetched(me, me) == h))
                put_weight(
                    0, 4 + h, wrap(sib - me), one_if(fetched(me, sib) == h)
                )
            return
        for t in (2 * group - 2, 2 * group - 1):
            dist = 1 if t < 4 else 2 if t < 8 else 3 if t < 11 else 4
            for side in range(2):
                for way in range(2):
                    home = me if side == 0 else sib
                    source = wrap(home - 2 * dist if way == 0 else home + 2 * dist)
                    if t < 8:
                        take = one_if(fetched(me, source) == t % 4)
                    elif t < 10:
                        take = one_if(core == t - 8)
                    elif t == 10:
                        take = 0.0
                    else:
                        take = float(side == way)
                    place = (t % 2) * 4 + side * 2 + way
                    put_weight(group, place, wrap(source - me), take)

    def multiply(q, group, read):
        @pl.loop(0, 3)
        def _(j):
            at = pl.multiple_of(j * 256, 256)
            xh, xl = split(read(at))
            dot = functools.partial(jnp.dot, preferred_element_type=F32)
            total = dot(wh[group], xh) + dot(wl[group], xh) + dot(wh[group], xl)
            if group == 0:
                acc[:, pl.ds(at, 256)] = total
            else:
                acc[:, pl.ds(at, 256)] += total

    def compute(q, group):
        if group == 0:
            multiply(
                q,
                0,
                lambda at: jnp.concatenate(
                    [xp[q, :, pl.ds(at, 256)], sibx[q, :, pl.ds(at, 256)]], axis=0
                ),
            )
        else:
            multiply(
                q,
                group,
                lambda at: pool[q, pl.ds(256 * (group - 1), 256), pl.ds(at, 256)],
            )

    def finish_chunk(q):
        for tile in range(6):
            cols = slice(tile * LANES, tile * LANES + LANES)
            total = jnp.zeros((128, LANES), F32)
            for order in range(4):
                factor = jnp.broadcast_to(kern[q, order, 0:1, cols], (128, LANES))
                total = total + acc[order * 128 : order * 128 + 128, cols] * factor
            cpl[q, :, cols] = total
        for k in range(1, DEV):
            coupled_copy(q, k).start()
        crecv[q, rad] = cpl[q, pl.ds(pl.multiple_of(8 * rad, 8), 8), :]

    def natural(piece):
        out = []
        for plane in range(2):
            cols = [slice((plane * 3 + i) * LANES, (plane * 3 + i + 1) * LANES) for i in range(3)]
            parts = [unpack4(*(piece(s, c) for c in cols)) for s in range(4)]
            for i in range(4):
                out.append(jnp.concatenate([p[i] for p in parts], axis=1))
        return out

    def kinetic_all():
        for k in range(1, DEV):
            state_copy(k).wait_recv()
        for q in range(Q):
            for quad in range(4):
                for i, value in enumerate(
                    natural(lambda s, c: srecv[4 * quad + s, q, :, c])
                ):
                    rows = slice(q * 64 + i * 8, q * 64 + i * 8 + 8)
                    snat[rows, 384 * quad : 384 * quad + 384] = value
        high = functools.partial(
            lax.dot_general, precision=lax.Precision.HIGHEST, preferred_element_type=F32
        )
        same = (((1,), (1,)), ((), ()))
        flip = (((1,), (0,)), ((), ()))
        for e in range(12):
            cols = [slice(128 * x, 128 * x + 128) for x in (e - 1, e, e + 1)]
            value = high(snat[:, cols[1]], diag_ref[e], same)
            if e > 0:
                value = value + high(snat[:, cols[0]], link_ref[e - 1], same)
            if e < 11:
                value = value + high(snat[:, cols[2]], link_ref[e], flip)
            app[:, cols[1]] = value

    def receive_coupled(q):
        for k in range(1, DEV):
            coupled_copy(q, k).wait_recv()
        for quad in range(4):
            for i, value in enumerate(
                natural(lambda s, c: crecv[q, 4 * quad + s, :, c])
            ):
                rows = pl.ds(pl.multiple_of(q * 64 + i * 8, 8), 8)
                cols = slice(384 * quad, 384 * quad + 384)
                app[rows, cols] += value

    def tail(q):
        arrived(q, 11)
        sib_arrived(q, 10)
        sib_arrived(q, 11)
        compute(q, 6)
        finish_chunk(q)

    build(0)
    sibx_copy.wait_recv()

    @pl.loop(0, Q)
    def _(q):
        nxt = q + 1
        more = q < Q - 1
        arrived(q, 0)
        ring_start(q, 4)
        arrived(q, 1)
        ring_start(q, 5)

        @pl.when(q > 0)
        def _():
            tail(q - 1)

        arrived(q, 2)
        ring_start(q, 6)
        arrived(q, 3)
        ring_start(q, 7)

        @pl.when(q == 0)
        def _():
            for group in range(1, 4):
                build(group)

        compute(q, 0)

        @pl.when(more)
        def _():
            ring_start(nxt, 0)
            ring_start(nxt, 1)

        sib_arrived(q, 0)
        sib_arrived(q, 1)
        compute(q, 1)
        for t in range(4, 8):
            arrived(q, t)
        for t in range(8, 11):
            ring_start(q, t)

        @pl.when(more)
        def _():
            ring_start(nxt, 2)
            ring_start(nxt, 3)

        @pl.when(q == 0)
        def _():
            for group in range(4, GROUPS):
                build(group)

        sib_arrived(q, 2)
        sib_arrived(q, 3)
        compute(q, 2)
        for t in range(8, 11):
            arrived(q, t)
        ring_start(q, 11)
        for t in range(4, 10):
            sib_arrived(q, t)
        for group in range(3, 6):
            compute(q, group)

        @pl.when(q == 0)
        def _():
            kinetic_all()

        @pl.when(q > 0)
        def _():
            receive_coupled(q - 1)

    tail(Q - 1)
    receive_coupled(Q - 1)

    def parts(q):
        re = pl.ds(q * 64, 32)
        im = pl.ds(q * 64 + 32, 32)
        return snat[re, :], snat[im, :], app[re, :], app[im, :]

    def fold(x):
        return jnp.sum(x, axis=0, keepdims=True)

    sums = [jnp.zeros((1, R), F32) for _ in range(3)]
    for q in range(Q):
        sre, sim, are, aim = parts(q)
        sums[0] += fold(sre * aim - sim * are)
        sums[1] -= fold(sre * are + sim * aim)
        sums[2] += fold(sre * sre + sim * sim)
    cross_re, cross_im, self_sq = (jnp.sum(x, axis=1, keepdims=True) for x in sums)

    def ratio(x, y):
        return jnp.where(y > 0.0, x / jnp.where(y > 0.0, y, 1.0), 0.0)

    own_re, own_im = ratio(cross_re, self_sq), ratio(cross_im, self_sq)
    left = jnp.zeros((1, R), F32)
    for q in range(Q):
        sre, sim, are, aim = parts(q)
        ore = aim - (own_re * sre - own_im * sim)
        oim = -are - (own_re * sim + own_im * sre)
        left += fold(ore * ore + oim * oim)
    left = jnp.sum(left, axis=1, keepdims=True)
    for i, value in enumerate((cross_re, cross_im, self_sq, left)):
        part[0, i : i + 1, :] = jnp.broadcast_to(value, (1, LANES))

    def scalar_copy(stage_, k):
        return pltpu.make_async_remote_copy(
            src_ref=part.at[stage_],
            dst_ref=gath.at[stage_, (me, rad)[stage_]],
            send_sem=sc_send.at[stage_, k],
            recv_sem=sc_recv.at[stage_, k],
            device_id=(chan_peer, rad_peer)[stage_](k),
            device_id_type=MESH,
        )

    def merge(stage_):
        for k in range(1, DEV):
            scalar_copy(stage_, k).start()
        gath[stage_, (me, rad)[stage_]] = part[stage_]
        for k in range(1, DEV):
            scalar_copy(stage_, k).wait_recv()
        rows = [[gath[stage_, j, i : i + 1, :] for j in range(DEV)] for i in range(4)]
        add = lambda xs: functools.reduce(lambda x, y: x + y, xs)
        cre, cim, sq = add(rows[0]), add(rows[1]), add(rows[2])
        pre, pim = ratio(cre, sq), ratio(cim, sq)
        rest = add(rows[3])
        for j in range(DEV):
            dre = pre - ratio(rows[0][j], rows[2][j])
            dim = pim - ratio(rows[1][j], rows[2][j])
            rest = rest + (dre * dre + dim * dim) * rows[2][j]
        return cre, cim, sq, rest, pre, pim

    merged = merge(0)
    for i in range(4):
        part[1, i : i + 1, :] = merged[i]
    _, _, _, rest, pre, pim = merge(1)
    rms = jnp.sqrt(rest / (2.0 * C * B * R) + 1e-06)
    coef_ref[0:1, :] = pre
    coef_ref[1:2, :] = pim
    coef_ref[2:3, :] = rms
    pre1, pim1 = pre[:, 0:1], pim[:, 0:1]
    for q in range(Q):
        for i in range(4):
            re = slice(q * 64 + i * 8, q * 64 + i * 8 + 8)
            im = slice(q * 64 + 32 + i * 8, q * 64 + 32 + i * 8 + 8)
            sre, sim, are, aim = snat[re, :], snat[im, :], app[re, :], app[im, :]
            ore = aim - (pre1 * sre - pim1 * sim)
            oim = -are - (pre1 * sim + pim1 * sre)
            for tile in range(R // LANES):
                cols = slice(tile * LANES, tile * LANES + LANES)
                rows = tile * 256 + 4 * q + i
                rows_of[pl.ds(rows, 8, stride=2 * B), :] = ore[:, cols]
                rows_of[pl.ds(rows + B, 8, stride=2 * B), :] = oim[:, cols]
    for tile in range(R // LANES):
        out_ref[:, tile * LANES : tile * LANES + LANES] = rows_of[tile * 256 : tile * 256 + 256, :]

    sibx_copy.wait_send()
    for k in range(1, DEV):
        state_copy(k).wait_send()
        scalar_copy(0, k).wait_send()
        scalar_copy(1, k).wait_send()

    @pl.loop(0, Q)
    def _(q):
        for t in range(T):
            for way in range(2):
                ring_copy(q, t, way, ring_src(q, t, way)).wait_send()
            sib_copy(q, t).wait_send()
        for k in range(1, DEV):
            coupled_copy(q, k).wait_send()


def per_device(
    state, coupling, fetch_group, live_slots, radius_one, radius_two, kinetic_diag, kinetic_link
):
    vmem = pl.BlockSpec(memory_space=pltpu.VMEM)
    smem = pl.BlockSpec(memory_space=pltpu.SMEM)
    dma = pltpu.SemaphoreType.DMA
    out, coef = pl.pallas_call(
        kernel,
        out_shape=(
            jax.ShapeDtypeStruct((8 * 2 * B, R), F32),
            jax.ShapeDtypeStruct((8, LANES), F32),
        ),
        in_specs=[vmem, vmem, smem, smem, smem, vmem, vmem, vmem],
        out_specs=(vmem, vmem),
        scratch_shapes=[
            pltpu.VMEM((Q, 128, CELLS), F32),
            pltpu.VMEM((Q, 128, CELLS), F32),
            pltpu.VMEM((Q, T * 4 * GS, CELLS), F32),
            pltpu.VMEM((Q, 6, GS, CELLS), F32),
            pltpu.VMEM((GROUPS, 512, 256), BF16),
            pltpu.VMEM((GROUPS, 512, 256), BF16),
            pltpu.VMEM((Q, 4, 8, CELLS), F32),
            pltpu.VMEM((512, CELLS), F32),
            pltpu.VMEM((Q, 128, CELLS), F32),
            pltpu.VMEM((DEV, Q, 8, CELLS), F32),
            pltpu.VMEM((Q, DEV, 8, CELLS), F32),
            pltpu.VMEM((256, R), F32),
            pltpu.VMEM((256, R), F32),
            pltpu.VMEM((R // LANES * 256, LANES), F32),
            pltpu.VMEM((2, 8, LANES), F32),
            pltpu.VMEM((2, DEV, 8, LANES), F32),
            dma((2, Q, T)),
            dma((2, Q, T)),
            dma((Q, T)),
            dma((Q, T)),
            dma((1,)),
            dma((1,)),
            dma((DEV,)),
            dma((DEV,)),
            dma((Q, DEV)),
            dma((Q, DEV)),
            dma((2, DEV)),
            dma((2, DEV)),
        ],
        compiler_params=pltpu.CompilerParams(
            collective_id=0, has_side_effects=True, vmem_limit_bytes=61 << 20
        ),
    )(
        state.reshape(128 * 2 * B, PTS),
        coupling.reshape(4 * 16 * 4 * GS, GS),
        fetch_group,
        live_slots,
        radius_one,
        radius_two.reshape(1, PTS),
        kinetic_diag,
        kinetic_link,
    )
    return out.reshape(8, 2, B, R), coef[0:3, 0]


def solution(mesh):
    placed = (
        P("chan", None, None, "rad"),
        P("chan", None, None, None, None),
        P(),
        P("chan"),
        P(),
        P("rad"),
        P(),
        P(),
    )
    return jax.shard_map(
        per_device,
        mesh=mesh,
        in_specs=placed,
        out_specs=(P(("chan", "rad"), None, None, None), P()),
        check_vma=False,
    )
```

```python
import functools

import jax
import jax.numpy as jnp
from jax import lax
from jax.experimental import pallas as pl
from jax.experimental.pallas import tpu as pltpu
from jax.sharding import PartitionSpec as P

MESH = pl.DeviceIdType.MESH
F32 = jnp.float32
BF16 = jnp.bfloat16

C = 2048
R = 1536
B = 16
DEV = 16
Q = 4
CELLS = 768
GS = 32
T = 9
GROUPS = 1 + (T + 1) // 2
LAG = 2
OCTETS = 16
STATIC_T = 12
STATIC_GROUPS = 1 + STATIC_T // 2
LANES = 128
PTS = 96


def split(x):
    high = x.astype(BF16)
    return high, (x - high.astype(F32)).astype(BF16)


def pack4(a, b, c, d):
    return (
        jnp.concatenate([a, d[:, 0:32]], axis=1),
        jnp.concatenate([b, d[:, 32:64]], axis=1),
        jnp.concatenate([c, d[:, 64:96]], axis=1),
    )


def unpack4(t0, t1, t2):
    last = jnp.concatenate([t0[:, 96:128], t1[:, 96:128], t2[:, 96:128]], axis=1)
    return t0[:, 0:96], t1[:, 0:96], t2[:, 0:96], last


def static_kernel(
    state_ref,
    coup_ref,
    fetch_ref,
    live_ref,
    r1_ref,
    r2_ref,
    diag_ref,
    link_ref,
    out_ref,
    coef_ref,
    xp,
    sibx,
    pool,
    stage,
    wh,
    wl,
    kern,
    acc,
    cpl,
    srecv,
    crecv,
    snat,
    app,
    rows_of,
    part,
    gath,
    ring_send,
    ring_recv,
    sib_send,
    sib_recv,
    sx_send,
    sx_recv,
    st_send,
    st_recv,
    cp_send,
    cp_recv,
    sc_send,
    sc_recv,
):
    me = lax.axis_index("chan")
    rad = lax.axis_index("rad")
    core = lax.rem(me, 2)
    sib = me + 1 - 2 * core
    up = (lax.rem(me + 2, DEV), rad)
    down = (lax.rem(me + DEV - 2, DEV), rad)
    sibling = (sib, rad)

    def chan_peer(k):
        return (lax.rem(me + k, DEV), rad)

    def rad_peer(k):
        return (me, lax.rem(rad + k, DEV))

    barrier = pltpu.get_barrier_semaphore()
    for k in range(1, DEV):
        pl.semaphore_signal(barrier, inc=1, device_id=chan_peer(k), device_id_type=MESH)
        pl.semaphore_signal(barrier, inc=1, device_id=rad_peer(k), device_id_type=MESH)

    for q in range(Q):
        for plane in range(2):
            rows = [
                state_ref[pl.ds(plane * B + 4 * q + i, 128, stride=2 * B), :]
                for i in range(4)
            ]
            for i, tile in enumerate(pack4(*rows)):
                at = (plane * 3 + i) * LANES
                xp[q, :, at : at + LANES] = tile

    pl.semaphore_wait(barrier, 2 * (DEV - 1))

    def slot(t, side, way):
        return (t * 4 + side * 2 + way) * GS

    def ring_copy(q, t, way, src):
        return pltpu.make_async_remote_copy(
            src_ref=src,
            dst_ref=pool.at[q, pl.ds(slot(t, 0, way), GS), :],
            send_sem=ring_send.at[way, q, t],
            recv_sem=ring_recv.at[way, q, t],
            device_id=(up, down)[way],
            device_id_type=MESH,
        )

    def ring_src(q, t, way):
        if t < 4:
            return xp.at[q, pl.ds(GS * t, GS), :]
        if t < 8:
            return pool.at[q, pl.ds(slot(t - 4, 0, way), GS), :]
        if t < 11:
            return stage.at[q, way * 3 + t - 8]
        return pool.at[q, pl.ds(slot(10, 0, way), GS), :]

    def fetched(dest, source):
        return fetch_ref[dest, source]

    def wrap(x):
        return lax.rem(x + 2 * DEV, DEV)

    picks = []
    for way in range(2):
        sign = 1 if way == 0 else -1
        source = wrap(me - 4 * sign)
        near = wrap(me - core + 2 * sign)
        far = wrap(me - core + 4 * sign)
        far_core = core if way == 0 else 1 - core
        picks.append(
            [
                fetched(near, source),
                fetched(near + 1, source),
                fetched(far + far_core, source),
            ]
        )

    def ring_start(q, t):
        for way in range(2):
            if 8 <= t < 11:
                pick = picks[way][t - 8]
                chosen = pool[q, pl.ds(slot(4, 0, way), GS), :]
                for h in range(1, 4):
                    chosen = jnp.where(
                        pick == h, pool[q, pl.ds(slot(4 + h, 0, way), GS), :], chosen
                    )
                stage[q, way * 3 + t - 8] = chosen
            ring_copy(q, t, way, ring_src(q, t, way)).start()

    def sib_copy(q, t):
        return pltpu.make_async_remote_copy(
            src_ref=pool.at[q, pl.ds(slot(t, 0, 0), 2 * GS), :],
            dst_ref=pool.at[q, pl.ds(slot(t, 1, 0), 2 * GS), :],
            send_sem=sib_send.at[q, t],
            recv_sem=sib_recv.at[q, t],
            device_id=sibling,
            device_id_type=MESH,
        )

    def arrived(q, t):
        for way in range(2):
            ring_copy(q, t, way, ring_src(q, t, way)).wait_recv()
        sib_copy(q, t).start()

    def sib_arrived(q, t):
        sib_copy(q, t).wait_recv()

    sibx_copy = pltpu.make_async_remote_copy(
        src_ref=xp,
        dst_ref=sibx,
        send_sem=sx_send.at[0],
        recv_sem=sx_recv.at[0],
        device_id=sibling,
        device_id_type=MESH,
    )

    def state_copy(k):
        return pltpu.make_async_remote_copy(
            src_ref=xp.at[:, pl.ds(8 * lax.rem(rad + k, DEV), 8), :],
            dst_ref=srecv.at[rad],
            send_sem=st_send.at[k],
            recv_sem=st_recv.at[k],
            device_id=rad_peer(k),
            device_id_type=MESH,
        )

    def coupled_copy(q, k):
        return pltpu.make_async_remote_copy(
            src_ref=cpl.at[q, pl.ds(8 * lax.rem(rad + k, DEV), 8), :],
            dst_ref=crecv.at[q, rad],
            send_sem=cp_send.at[q, k],
            recv_sem=cp_recv.at[q, k],
            device_id=rad_peer(k),
            device_id_type=MESH,
        )

    ring_start(0, 0)
    ring_start(0, 1)
    sibx_copy.start()
    for k in range(1, DEV):
        state_copy(k).start()
    ring_start(0, 2)
    ring_start(0, 3)
    srecv[rad] = xp[:, pl.ds(pl.multiple_of(8 * rad, 8), 8), :]

    row = jnp.broadcast_to(r2_ref[0:1, :], (8, PTS))
    tails = pack4(row, row, row, row)
    lane = lax.broadcasted_iota(jnp.int32, (8, LANES), 1)
    for q in range(Q):
        for i in range(3):
            one = jnp.where(lane < PTS, r1_ref[4 * q + i], r1_ref[4 * q + 3])
            nearer = jnp.minimum(one, tails[i])
            farther = jnp.maximum(one, tails[i])
            top = jnp.ones_like(nearer)
            bottom = farther
            for order in range(4):
                value = top / bottom
                for plane in range(2):
                    at = (plane * 3 + i) * LANES
                    kern[q, order, :, at : at + LANES] = value
                top = top * nearer
                bottom = bottom * farther

    def put_weight(group, place, k, take):
        for g in range(4):
            on = jnp.where(live_ref[g] > k, take, 0.0)
            for order in range(4):
                start = ((g * 16 + k) * 4 + order) * GS
                block = coup_ref[pl.ds(pl.multiple_of(start, GS), GS), :] * on
                high, low = split(block)
                rows = slice(order * 128 + g * GS, order * 128 + g * GS + GS)
                cols = slice(place * GS, place * GS + GS)
                wh[group, rows, cols] = high
                wl[group, rows, cols] = low

    def one_if(condition):
        return jnp.where(condition, 1.0, 0.0)

    def build(group):
        if group == 0:
            for h in range(4):
                put_weight(0, h, 0, one_if(fetched(me, me) == h))
                put_weight(
                    0, 4 + h, wrap(sib - me), one_if(fetched(me, sib) == h)
                )
            return
        for t in (2 * group - 2, 2 * group - 1):
            dist = 1 if t < 4 else 2 if t < 8 else 3 if t < 11 else 4
            for side in range(2):
                for way in range(2):
                    home = me if side == 0 else sib
                    source = wrap(home - 2 * dist if way == 0 else home + 2 * dist)
                    if t < 8:
                        take = one_if(fetched(me, source) == t % 4)
                    elif t < 10:
                        take = one_if(core == t - 8)
                    elif t == 10:
                        take = 0.0
                    else:
                        take = float(side == way)
                    place = (t % 2) * 4 + side * 2 + way
                    put_weight(group, place, wrap(source - me), take)

    def multiply(q, group, read):
        @pl.loop(0, 3)
        def _(j):
            at = pl.multiple_of(j * 256, 256)
            xh, xl = split(read(at))
            dot = functools.partial(jnp.dot, preferred_element_type=F32)
            total = dot(wh[group], xh) + dot(wl[group], xh) + dot(wh[group], xl)
            if group == 0:
                acc[:, pl.ds(at, 256)] = total
            else:
                acc[:, pl.ds(at, 256)] += total

    def compute(q, group):
        if group == 0:
            multiply(
                q,
                0,
                lambda at: jnp.concatenate(
                    [xp[q, :, pl.ds(at, 256)], sibx[q, :, pl.ds(at, 256)]], axis=0
                ),
            )
        else:
            multiply(
                q,
                group,
                lambda at: pool[q, pl.ds(256 * (group - 1), 256), pl.ds(at, 256)],
            )

    def finish_chunk(q):
        for tile in range(6):
            cols = slice(tile * LANES, tile * LANES + LANES)
            total = jnp.zeros((128, LANES), F32)
            for order in range(4):
                factor = jnp.broadcast_to(kern[q, order, 0:1, cols], (128, LANES))
                total = total + acc[order * 128 : order * 128 + 128, cols] * factor
            cpl[q, :, cols] = total
        for k in range(1, DEV):
            coupled_copy(q, k).start()
        crecv[q, rad] = cpl[q, pl.ds(pl.multiple_of(8 * rad, 8), 8), :]

    def natural(piece):
        out = []
        for plane in range(2):
            cols = [slice((plane * 3 + i) * LANES, (plane * 3 + i + 1) * LANES) for i in range(3)]
            parts = [unpack4(*(piece(s, c) for c in cols)) for s in range(4)]
            for i in range(4):
                out.append(jnp.concatenate([p[i] for p in parts], axis=1))
        return out

    def kinetic_all():
        for k in range(1, DEV):
            state_copy(k).wait_recv()
        for q in range(Q):
            for quad in range(4):
                for i, value in enumerate(
                    natural(lambda s, c: srecv[4 * quad + s, q, :, c])
                ):
                    rows = slice(q * 64 + i * 8, q * 64 + i * 8 + 8)
                    snat[rows, 384 * quad : 384 * quad + 384] = value
        high = functools.partial(
            lax.dot_general, precision=lax.Precision.HIGHEST, preferred_element_type=F32
        )
        same = (((1,), (1,)), ((), ()))
        flip = (((1,), (0,)), ((), ()))
        for e in range(12):
            cols = [slice(128 * x, 128 * x + 128) for x in (e - 1, e, e + 1)]
            value = high(snat[:, cols[1]], diag_ref[e], same)
            if e > 0:
                value = value + high(snat[:, cols[0]], link_ref[e - 1], same)
            if e < 11:
                value = value + high(snat[:, cols[2]], link_ref[e], flip)
            app[:, cols[1]] = value

    def receive_coupled(q):
        for k in range(1, DEV):
            coupled_copy(q, k).wait_recv()
        for quad in range(4):
            for i, value in enumerate(
                natural(lambda s, c: crecv[q, 4 * quad + s, :, c])
            ):
                rows = pl.ds(pl.multiple_of(q * 64 + i * 8, 8), 8)
                cols = slice(384 * quad, 384 * quad + 384)
                app[rows, cols] += value

    def tail(q):
        arrived(q, 11)
        sib_arrived(q, 10)
        sib_arrived(q, 11)
        compute(q, 6)
        finish_chunk(q)

    build(0)
    sibx_copy.wait_recv()

    @pl.loop(0, Q)
    def _(q):
        nxt = q + 1
        more = q < Q - 1
        arrived(q, 0)
        ring_start(q, 4)
        arrived(q, 1)
        ring_start(q, 5)

        @pl.when(q > 0)
        def _():
            tail(q - 1)

        arrived(q, 2)
        ring_start(q, 6)
        arrived(q, 3)
        ring_start(q, 7)

        @pl.when(q == 0)
        def _():
            for group in range(1, 4):
                build(group)

        compute(q, 0)

        @pl.when(more)
        def _():
            ring_start(nxt, 0)
            ring_start(nxt, 1)

        sib_arrived(q, 0)
        sib_arrived(q, 1)
        compute(q, 1)
        for t in range(4, 8):
            arrived(q, t)
        for t in range(8, 11):
            ring_start(q, t)

        @pl.when(more)
        def _():
            ring_start(nxt, 2)
            ring_start(nxt, 3)

        @pl.when(q == 0)
        def _():
            for group in range(4, STATIC_GROUPS):
                build(group)

        sib_arrived(q, 2)
        sib_arrived(q, 3)
        compute(q, 2)
        for t in range(8, 11):
            arrived(q, t)
        ring_start(q, 11)
        for t in range(4, 10):
            sib_arrived(q, t)
        for group in range(3, 6):
            compute(q, group)

        @pl.when(q == 0)
        def _():
            kinetic_all()

        @pl.when(q > 0)
        def _():
            receive_coupled(q - 1)

    tail(Q - 1)
    receive_coupled(Q - 1)

    def parts(q):
        re = pl.ds(q * 64, 32)
        im = pl.ds(q * 64 + 32, 32)
        return snat[re, :], snat[im, :], app[re, :], app[im, :]

    def fold(x):
        return jnp.sum(x, axis=0, keepdims=True)

    sums = [jnp.zeros((1, R), F32) for _ in range(3)]
    for q in range(Q):
        sre, sim, are, aim = parts(q)
        sums[0] += fold(sre * aim - sim * are)
        sums[1] -= fold(sre * are + sim * aim)
        sums[2] += fold(sre * sre + sim * sim)
    cross_re, cross_im, self_sq = (jnp.sum(x, axis=1, keepdims=True) for x in sums)

    def ratio(x, y):
        return jnp.where(y > 0.0, x / jnp.where(y > 0.0, y, 1.0), 0.0)

    own_re, own_im = ratio(cross_re, self_sq), ratio(cross_im, self_sq)
    left = jnp.zeros((1, R), F32)
    for q in range(Q):
        sre, sim, are, aim = parts(q)
        ore = aim - (own_re * sre - own_im * sim)
        oim = -are - (own_re * sim + own_im * sre)
        left += fold(ore * ore + oim * oim)
    left = jnp.sum(left, axis=1, keepdims=True)
    for i, value in enumerate((cross_re, cross_im, self_sq, left)):
        part[0, i : i + 1, :] = jnp.broadcast_to(value, (1, LANES))

    def scalar_copy(stage_, k):
        return pltpu.make_async_remote_copy(
            src_ref=part.at[stage_],
            dst_ref=gath.at[stage_, (me, rad)[stage_]],
            send_sem=sc_send.at[stage_, k],
            recv_sem=sc_recv.at[stage_, k],
            device_id=(chan_peer, rad_peer)[stage_](k),
            device_id_type=MESH,
        )

    def merge(stage_):
        for k in range(1, DEV):
            scalar_copy(stage_, k).start()
        gath[stage_, (me, rad)[stage_]] = part[stage_]
        for k in range(1, DEV):
            scalar_copy(stage_, k).wait_recv()
        rows = [[gath[stage_, j, i : i + 1, :] for j in range(DEV)] for i in range(4)]
        add = lambda xs: functools.reduce(lambda x, y: x + y, xs)
        cre, cim, sq = add(rows[0]), add(rows[1]), add(rows[2])
        pre, pim = ratio(cre, sq), ratio(cim, sq)
        rest = add(rows[3])
        for j in range(DEV):
            dre = pre - ratio(rows[0][j], rows[2][j])
            dim = pim - ratio(rows[1][j], rows[2][j])
            rest = rest + (dre * dre + dim * dim) * rows[2][j]
        return cre, cim, sq, rest, pre, pim

    merged = merge(0)
    for i in range(4):
        part[1, i : i + 1, :] = merged[i]
    _, _, _, rest, pre, pim = merge(1)
    rms = jnp.sqrt(rest / (2.0 * C * B * R) + 1e-06)
    coef_ref[0:1, :] = pre
    coef_ref[1:2, :] = pim
    coef_ref[2:3, :] = rms
    pre1, pim1 = pre[:, 0:1], pim[:, 0:1]
    for q in range(Q):
        for i in range(4):
            re = slice(q * 64 + i * 8, q * 64 + i * 8 + 8)
            im = slice(q * 64 + 32 + i * 8, q * 64 + 32 + i * 8 + 8)
            sre, sim, are, aim = snat[re, :], snat[im, :], app[re, :], app[im, :]
            ore = aim - (pre1 * sre - pim1 * sim)
            oim = -are - (pre1 * sim + pim1 * sre)
            for tile in range(R // LANES):
                cols = slice(tile * LANES, tile * LANES + LANES)
                rows = tile * 256 + 4 * q + i
                rows_of[pl.ds(rows, 8, stride=2 * B), :] = ore[:, cols]
                rows_of[pl.ds(rows + B, 8, stride=2 * B), :] = oim[:, cols]
    for tile in range(R // LANES):
        out_ref[:, tile * LANES : tile * LANES + LANES] = rows_of[tile * 256 : tile * 256 + 256, :]

    sibx_copy.wait_send()
    for k in range(1, DEV):
        state_copy(k).wait_send()
        scalar_copy(0, k).wait_send()
        scalar_copy(1, k).wait_send()

    @pl.loop(0, Q)
    def _(q):
        for t in range(STATIC_T):
            for way in range(2):
                ring_copy(q, t, way, ring_src(q, t, way)).wait_send()
            sib_copy(q, t).wait_send()
        for k in range(1, DEV):
            coupled_copy(q, k).wait_send()


def static_program(
    state, coupling, fetch_group, live_slots, radius_one, radius_two, kinetic_diag, kinetic_link
):
    vmem = pl.BlockSpec(memory_space=pltpu.VMEM)
    smem = pl.BlockSpec(memory_space=pltpu.SMEM)
    dma = pltpu.SemaphoreType.DMA
    out, coef = pl.pallas_call(
        static_kernel,
        out_shape=(
            jax.ShapeDtypeStruct((8 * 2 * B, R), F32),
            jax.ShapeDtypeStruct((8, LANES), F32),
        ),
        in_specs=[vmem, vmem, smem, smem, smem, vmem, vmem, vmem],
        out_specs=(vmem, vmem),
        scratch_shapes=[
            pltpu.VMEM((Q, 128, CELLS), F32),
            pltpu.VMEM((Q, 128, CELLS), F32),
            pltpu.VMEM((Q, STATIC_T * 4 * GS, CELLS), F32),
            pltpu.VMEM((Q, 6, GS, CELLS), F32),
            pltpu.VMEM((STATIC_GROUPS, 512, 256), BF16),
            pltpu.VMEM((STATIC_GROUPS, 512, 256), BF16),
            pltpu.VMEM((Q, 4, 8, CELLS), F32),
            pltpu.VMEM((512, CELLS), F32),
            pltpu.VMEM((Q, 128, CELLS), F32),
            pltpu.VMEM((DEV, Q, 8, CELLS), F32),
            pltpu.VMEM((Q, DEV, 8, CELLS), F32),
            pltpu.VMEM((256, R), F32),
            pltpu.VMEM((256, R), F32),
            pltpu.VMEM((R // LANES * 256, LANES), F32),
            pltpu.VMEM((2, 8, LANES), F32),
            pltpu.VMEM((2, DEV, 8, LANES), F32),
            dma((2, Q, STATIC_T)),
            dma((2, Q, STATIC_T)),
            dma((Q, STATIC_T)),
            dma((Q, STATIC_T)),
            dma((1,)),
            dma((1,)),
            dma((DEV,)),
            dma((DEV,)),
            dma((Q, DEV)),
            dma((Q, DEV)),
            dma((2, DEV)),
            dma((2, DEV)),
        ],
        compiler_params=pltpu.CompilerParams(
            collective_id=1, has_side_effects=True, vmem_limit_bytes=61 << 20
        ),
    )(
        state.reshape(128 * 2 * B, PTS),
        coupling.reshape(4 * 16 * 4 * GS, GS),
        fetch_group,
        live_slots,
        radius_one,
        radius_two.reshape(1, PTS),
        kinetic_diag,
        kinetic_link,
    )
    return out.reshape(8, 2, B, R), coef[0:3, 0]


def tie_up(v, dest_z, dest_core, source_core):
    index = dest_z * 4 + dest_core * 2 + source_core
    mixed = (((v * 5 + 3) * (index + 1) * (index + 7)) >> 3) & 1
    odd = (dest_core + source_core) & 1
    return jnp.where(
        v == 0,
        1 - odd,
        jnp.where(v == 1, odd, jnp.where(v == 2, 1 - source_core, jnp.where(v == 3, source_core, mixed))),
    )


def flat4(t0, t1, t2):
    return (
        t0[:, 0:96],
        jnp.concatenate([t0[:, 96:128], t1[:, 0:64]], axis=1),
        jnp.concatenate([t1[:, 64:128], t2[:, 0:32]], axis=1),
        t2[:, 32:128],
    )


def kernel(
    state_hbm,
    coup_hbm,
    fetch_ref,
    live_ref,
    r1_ref,
    r2_ref,
    diag_hbm,
    link_hbm,
    out_ref,
    coef_ref,
    flag_ref,
    state_v,
    coup_v,
    diag_v,
    link_v,
    xb,
    pool,
    stage,
    ch,
    cl,
    wh,
    wl,
    kern,
    acc,
    cpl,
    srecv,
    crecv,
    snat,
    app,
    rows_of,
    part,
    gath,
    live_out,
    live_in,
    sim_key,
    sim_read,
    read_table,
    slot_table,
    load_sem,
    live_send,
    live_recv,
    ring_send,
    ring_recv,
    sib_send,
    sib_recv,
    sx_send,
    sx_recv,
    st_send,
    st_recv,
    cp_send,
    cp_recv,
    sc_send,
    sc_recv,
):
    me = lax.axis_index("chan")
    rad = lax.axis_index("rad")
    core = lax.rem(me, 2)
    chip = me // 2
    sib = me + 1 - 2 * core
    up = (lax.rem(me + 2, DEV), rad)
    down = (lax.rem(me + DEV - 2, DEV), rad)
    sibling = (sib, rad)

    def chan_peer(k):
        return (lax.rem(me + k, DEV), rad)

    def rad_peer(k):
        return (me, lax.rem(rad + k, DEV))

    loads = [
        pltpu.make_async_copy(src, dst, load_sem.at[i])
        for i, (src, dst) in enumerate(
            ((state_hbm, state_v), (coup_hbm, coup_v), (diag_hbm, diag_v), (link_hbm, link_v))
        )
    ]
    for load in loads:
        load.start()
    barrier = pltpu.get_barrier_semaphore()
    for k in range(1, DEV):
        pl.semaphore_signal(barrier, inc=1, device_id=chan_peer(k), device_id_type=MESH)
        pl.semaphore_signal(barrier, inc=1, device_id=rad_peer(k), device_id_type=MESH)

    mine = jnp.maximum(
        jnp.maximum(live_ref[0], live_ref[1]), jnp.maximum(live_ref[2], live_ref[3])
    )
    live_out[...] = jnp.full((8, LANES), mine, jnp.int32)

    lane = lax.broadcasted_iota(jnp.int32, (8, LANES), 1)
    sub = lax.broadcasted_iota(jnp.int32, (8, LANES), 0)
    lane_z = lane & 7
    octet = lane >> 3
    sub_core = sub >> 2
    sub_block = sub & 3
    spots = [[(lane_z == z) & (sub_core == s) for s in range(2)] for z in range(8)]
    taken = {}
    for delta in range(1, 8):
        for dest_core in range(2):
            value = jnp.zeros((8, LANES), jnp.int32)
            for z in range(8):
                for s in range(2):
                    picked = fetch_ref[2 * ((z + delta) % 8) + dest_core, 2 * z + s]
                    value = jnp.where(spots[z][s], picked, value)
            taken[delta, dest_core] = value == sub_block

    def live_copy(k):
        return pltpu.make_async_remote_copy(
            src_ref=live_out,
            dst_ref=live_in.at[me],
            send_sem=live_send.at[k],
            recv_sem=live_recv.at[k],
            device_id=chan_peer(k),
            device_id_type=MESH,
        )

    def sibx_copy(q):
        return pltpu.make_async_remote_copy(
            src_ref=xb.at[core, q],
            dst_ref=xb.at[core, q],
            send_sem=sx_send.at[q],
            recv_sem=sx_recv.at[q],
            device_id=sibling,
            device_id_type=MESH,
        )

    def state_copy(k):
        return pltpu.make_async_remote_copy(
            src_ref=xb.at[core, :, pl.ds(8 * lax.rem(rad + k, DEV), 8), :],
            dst_ref=srecv.at[rad],
            send_sem=st_send.at[k],
            recv_sem=st_recv.at[k],
            device_id=rad_peer(k),
            device_id_type=MESH,
        )

    def coupled_copy(q, k):
        return pltpu.make_async_remote_copy(
            src_ref=cpl.at[q, pl.ds(8 * lax.rem(rad + k, DEV), 8), :],
            dst_ref=crecv.at[q, rad],
            send_sem=cp_send.at[q, k],
            recv_sem=cp_recv.at[q, k],
            device_id=rad_peer(k),
            device_id_type=MESH,
        )

    def slot(t, side, way):
        return pl.multiple_of((t * 4 + side * 2 + way) * GS, GS)

    def ring_copy(q, t, way):
        return pltpu.make_async_remote_copy(
            src_ref=stage.at[way, q, t],
            dst_ref=pool.at[q, pl.ds(slot(t, core, way), GS), :],
            send_sem=ring_send.at[way, q, t],
            recv_sem=ring_recv.at[way, q, t],
            device_id=(up, down)[way],
            device_id_type=MESH,
        )

    def sib_copy(q, t):
        return pltpu.make_async_remote_copy(
            src_ref=pool.at[q, pl.ds(slot(t, core, 0), 2 * GS), :],
            dst_ref=pool.at[q, pl.ds(slot(t, core, 0), 2 * GS), :],
            send_sem=sib_send.at[q, t],
            recv_sem=sib_recv.at[q, t],
            device_id=sibling,
            device_id_type=MESH,
        )

    pl.semaphore_wait(barrier, 2 * (DEV - 1))
    for k in range(1, DEV):
        live_copy(k).start()
    live_in[me] = live_out[...]

    loads[0].wait()
    for q in range(Q):
        for plane in range(2):
            rows = slice(plane * B * PTS + 384 * q, plane * B * PTS + 384 * q + 384)
            xb[core, q, :, plane * 384 : plane * 384 + 384] = jnp.transpose(state_v[rows, :])
        sibx_copy(q).start()
    for k in range(1, DEV):
        state_copy(k).start()
    srecv[rad] = xb[core, :, pl.ds(pl.multiple_of(8 * rad, 8), 8), :]

    for k in range(1, DEV):
        live_copy(k).wait_recv()
    most = []
    for dest_core in range(2):
        value = live_in[dest_core]
        for z in range(1, 8):
            value = jnp.where(lane_z == z, live_in[2 * z + dest_core], value)
        most.append(value)

    def turn(x, shift):
        shift = shift % 8
        if shift == 0:
            return x
        return jnp.where(
            lane_z >= shift,
            pltpu.roll(x, shift, 1),
            pltpu.roll(x, LANES - 8 + shift, 1),
        )

    reach = []
    for way in range(2):
        value = jnp.zeros((8, LANES), jnp.int32)
        for dist in range(1, 5):
            delta = dist if way == 0 else 8 - dist
            for dest_core in range(2):
                k = ((2 * dist if way else -2 * dist) + sub_core - dest_core) & 15
                need = taken[delta, dest_core] & (
                    k < pltpu.roll(most[dest_core], LANES - delta, 1)
                )
                if dist == 4:
                    upward = tie_up(octet, (lane_z + 4) & 7, dest_core, sub_core)
                    need = need & (upward == 1 - way)
                value = jnp.where(need, dist, value)
        reach.append(value)

    waiting, ready, where_from = [], [], []
    for way in range(2):
        here = [turn(reach[way], j if way == 0 else -j) for j in range(4)]
        waiting.append(
            [jnp.where(r > j, (r - j) * 32 + j * 8 + sub, 0) for j, r in enumerate(here)]
        )
        ready.append([jnp.full((8, LANES), 0 if j == 0 else 99, jnp.int32) for j in range(4)])
        where_from.append([sub for _ in range(4)])

    def peak(x):
        for shift in (4, 2, 1):
            x = jnp.maximum(x, pltpu.roll(x, shift, 0))
        return x

    sim_key[...] = jnp.zeros(sim_key.shape, jnp.int32)
    sim_read[...] = jnp.zeros(sim_read.shape, jnp.int32)
    for t in range(T):
        for way in range(2):
            wait, soon, source = waiting[way], ready[way], where_from[way]
            sent = [jnp.zeros((8, LANES), jnp.int32) for _ in range(4)]
            for side in range(2):
                open_ = [
                    jnp.where((soon[j] <= t) & (sent[j] == 0), wait[j], 0) for j in range(4)
                ]
                top = peak(functools.reduce(jnp.maximum, open_))
                chosen = [(open_[j] == top) & (top > 0) for j in range(4)]
                code = peak(
                    functools.reduce(
                        jnp.maximum,
                        [jnp.where(chosen[j], source[j] + 1, 0) for j in range(4)],
                    )
                )
                row = t * 4 + side * 2 + way
                sim_key[row : row + 1, :] = top[0:1, :]
                sim_read[row : row + 1, :] = code[0:1, :]
                sent = [jnp.where(chosen[j], side + 1, sent[j]) for j in range(4)]
            waiting[way] = [jnp.where(sent[j] > 0, 0, wait[j]) for j in range(4)]
            for j in range(3):
                came = turn(sent[j], 1 if way == 0 else -1)
                soon[j + 1] = jnp.where(came > 0, t + LAG, soon[j + 1])
                source[j + 1] = jnp.where(came > 0, 8 + 2 * t - 1 + came, source[j + 1])

    left = peak(functools.reduce(jnp.maximum, waiting[0] + waiting[1]))
    for shift in (4, 2, 1):
        left = jnp.maximum(left, turn(left, shift))
    routing = jnp.min(
        jnp.where(left > 0, 99.0, octet.astype(F32)), axis=1, keepdims=True
    )
    flag_ref[0] = jnp.where(jnp.max(routing) > 50.0, 1, 0)
    routing = jnp.where(routing > 50.0, 0.0, routing).astype(jnp.int32)[0:1, :]

    rows_n = sim_key.shape[0]
    wide = lax.broadcasted_iota(jnp.int32, (rows_n, LANES), 1)
    tall = lax.broadcasted_iota(jnp.int32, (rows_n, LANES), 0)

    def column(table, z):
        hit = wide == routing * 8 + z
        picked = jnp.where(hit, table.astype(F32), 0.0)
        return jnp.broadcast_to(
            jnp.sum(picked, axis=1, keepdims=True), (rows_n, LANES)
        ).astype(jnp.int32)

    read_table[...] = column(sim_read[...], chip)
    came_way = tall & 1
    key = column(
        sim_key[...], jnp.where(came_way == 0, (chip + 7) & 7, (chip + 1) & 7)
    )
    ident = key & 31
    dist = (ident >> 3) + 1
    from_core = (ident >> 2) & 1
    from_block = ident & 3
    k = (jnp.where(came_way == 0, -2 * dist, 2 * dist) + from_core - core) & 15
    fetched = jnp.zeros_like(k)
    for j in range(DEV):
        fetched = jnp.where(k == j, fetch_ref[me, lax.rem(me + j, DEV)], fetched)
    upward = tie_up(jnp.broadcast_to(routing, (rows_n, LANES)), chip, core, from_core)
    take = (key > 0) & (fetched == from_block) & (tall < 4 * T)
    take = take & ((dist < 4) | (upward == 1 - came_way))
    slot_table[8 : 8 + rows_n, :] = jnp.where(take, k, -1)
    own = jnp.where(
        sub_core == 0,
        fetch_ref[me, me - core],
        fetch_ref[me, me - core + 1],
    )
    slot_table[0:8, :] = jnp.where(own == sub_block, (sub_core - core) & 15, -1)

    def ring_start(q, t):
        for way in range(2):
            row = t * 4 + way
            code = jnp.where(
                jnp.full((1, LANES), core, jnp.int32) == 0,
                read_table[row : row + 1, :],
                read_table[row + 2 : row + 3, :],
            )
            code = jnp.broadcast_to(code, (GS, LANES))
            tiles = [slice(i * LANES, i * LANES + LANES) for i in range(6)]
            chosen = [xb[0, q, 0:GS, c] for c in tiles]
            for i in range(1, 8 + 2 * max(0, t - LAG + 1)):
                hit = code == i + 1
                for n, c in enumerate(tiles):
                    if i < 8:
                        rows = pl.ds((i % 4) * GS, GS)
                        block = xb[i // 4, q, rows, c]
                    else:
                        block = pool[q, pl.ds(slot((i - 8) // 2, i % 2, way), GS), c]
                    chosen[n] = jnp.where(hit, block, chosen[n])
            for n, c in enumerate(tiles):
                stage[way, q, t, :, c] = chosen[n]
            ring_copy(q, t, way).start()

    def ring_arrived(q, t):
        for way in range(2):
            ring_copy(q, t, way).wait_recv()
        sib_copy(q, t).start()

    def sib_arrived(q, t):
        sib_copy(q, t).wait_recv()

    def build_coupling():
        loads[1].wait()
        for g in range(4):
            for four in range(4):
                on = [
                    jnp.where(live_ref[g] > 4 * four + j, 1.0, 0.0) for j in range(4)
                ]
                for order in range(4):
                    block = jnp.concatenate(
                        [
                            coup_v[pl.ds(((g * 16 + 4 * four + j) * 4 + order) * GS, GS), :]
                            * on[j]
                            for j in range(4)
                        ],
                        axis=1,
                    )
                    high, low = split(block)
                    rows = slice(order * 128 + g * GS, order * 128 + g * GS + GS)
                    cols = slice(four * LANES, four * LANES + LANES)
                    ch[rows, cols] = high
                    cl[rows, cols] = low

    def build(group):
        width = 256 if group < GROUPS - 1 or T % 2 == 0 else 128
        depth = lax.broadcasted_iota(jnp.int32, (512, LANES), 0)
        across = lax.broadcasted_iota(jnp.int32, (1, LANES), 1)
        for half in range(width // 128):
            target = jnp.full((1, LANES), -1, jnp.int32)
            for p in range(4):
                row = 8 * group + 4 * half + p
                target = jnp.where(across >> 5 == p, slot_table[row : row + 1, :], target)
            target = target * GS + (across & 31)
            select = jnp.where(depth == target, 1.0, 0.0).astype(BF16)
            cols = slice(half * 128, half * 128 + 128)
            for src, dst in ((ch, wh), (cl, wl)):
                dst[group, :, cols] = jnp.dot(
                    src[...], select, preferred_element_type=F32
                ).astype(BF16)

    def compute(q, group):
        half = lax.rem(q, 2)
        width = 256 if group < GROUPS - 1 or T % 2 == 0 else 128

        @pl.loop(0, 3)
        def _(j):
            at = pl.multiple_of(j * 256, 256)
            if group == 0:
                x = jnp.concatenate(
                    [xb[0, q, :, pl.ds(at, 256)], xb[1, q, :, pl.ds(at, 256)]], axis=0
                )
            else:
                x = pool[q, pl.ds(256 * (group - 1), width), pl.ds(at, 256)]
            xh, xl = split(x)
            dot = functools.partial(jnp.dot, preferred_element_type=F32)
            gh, gl = wh[group, :, 0:width], wl[group, :, 0:width]
            total = dot(gh, xh) + dot(gl, xh) + dot(gh, xl)
            if group == 0:
                acc[half, :, pl.ds(at, 256)] = total
            else:
                acc[half, :, pl.ds(at, 256)] += total

    def build_kern():
        row = jnp.broadcast_to(r2_ref[0:1, :], (8, PTS))
        flat = jnp.concatenate([row] * 4, axis=1)
        point = lax.broadcasted_iota(jnp.int32, (8, 384), 1)
        for q in range(Q):
            one = jnp.where(
                point < PTS,
                r1_ref[4 * q],
                jnp.where(
                    point < 2 * PTS,
                    r1_ref[4 * q + 1],
                    jnp.where(point < 3 * PTS, r1_ref[4 * q + 2], r1_ref[4 * q + 3]),
                ),
            )
            nearer = jnp.minimum(one, flat)
            farther = jnp.maximum(one, flat)
            top = jnp.ones_like(nearer)
            bottom = farther
            for order in range(4):
                value = top / bottom
                kern[q, order, :, 0:384] = value
                kern[q, order, :, 384:768] = value
                top = top * nearer
                bottom = bottom * farther

    def finish_chunk(q):
        half = lax.rem(q, 2)
        for tile in range(6):
            cols = slice(tile * LANES, tile * LANES + LANES)
            total = jnp.zeros((128, LANES), F32)
            for order in range(4):
                factor = jnp.broadcast_to(kern[q, order, 0:1, cols], (128, LANES))
                total = total + acc[half, order * 128 : order * 128 + 128, cols] * factor
            cpl[q, :, cols] = total
        for k in range(1, DEV):
            coupled_copy(q, k).start()
        crecv[q, rad] = cpl[q, pl.ds(pl.multiple_of(8 * rad, 8), 8), :]

    def natural(piece):
        out = []
        for plane in range(2):
            cols = [slice((plane * 3 + i) * LANES, (plane * 3 + i + 1) * LANES) for i in range(3)]
            parts = [flat4(*(piece(s, c) for c in cols)) for s in range(4)]
            for i in range(4):
                out.append(jnp.concatenate([p[i] for p in parts], axis=1))
        return out

    def receive_state():
        for k in range(1, DEV):
            state_copy(k).wait_recv()
        for q in range(Q):
            for quad in range(4):
                for i, value in enumerate(
                    natural(lambda s, c: srecv[4 * quad + s, q, :, c])
                ):
                    rows = slice(q * 64 + i * 8, q * 64 + i * 8 + 8)
                    snat[rows, 384 * quad : 384 * quad + 384] = value

    def kinetic(elements):
        high = functools.partial(
            lax.dot_general, precision=lax.Precision.HIGHEST, preferred_element_type=F32
        )
        same = (((1,), (1,)), ((), ()))
        flip = (((1,), (0,)), ((), ()))
        for e in elements:
            cols = [slice(128 * x, 128 * x + 128) for x in (e - 1, e, e + 1)]
            value = high(snat[:, cols[1]], diag_v[e], same)
            if e > 0:
                value = value + high(snat[:, cols[0]], link_v[e - 1], same)
            if e < 11:
                value = value + high(snat[:, cols[2]], link_v[e], flip)
            app[:, cols[1]] = value

    def receive_coupled(q):
        for k in range(1, DEV):
            coupled_copy(q, k).wait_recv()
        for quad in range(4):
            for i, value in enumerate(
                natural(lambda s, c: crecv[q, 4 * quad + s, :, c])
            ):
                rows = pl.ds(pl.multiple_of(q * 64 + i * 8, 8), 8)
                cols = slice(384 * quad, 384 * quad + 384)
                app[rows, cols] += value

    for q in range(Q):
        sibx_copy(q).wait_recv()

    def chunk_round(n):
        return 2 * (n // (2 * T)) + lax.rem(n, 2), lax.rem(n, 2 * T) // 2

    @pl.loop(0, Q // 2)
    def _(pair):
        for t in range(T):

            @pl.loop(0, 2)
            def _(parity):
                q = 2 * pair + parity
                last = q - 2
                n = 2 * T * pair + 2 * t + parity

                @pl.when(n >= 3)
                def _():
                    ring_arrived(*chunk_round(n - 3))

                @pl.when(n >= 4)
                def _():
                    sib_arrived(*chunk_round(n - 4))

                ring_start(q, t)

                if t == 0:

                    @pl.when(q == 0)
                    def _():
                        build_coupling()

                if t == 1:

                    @pl.when(q == 0)
                    def _():
                        build(0)
                        build(1)

                    @pl.when(q == 1)
                    def _():
                        build_kern()

                if t < LAG and (T + t) % 2 and (T + t) // 2 < GROUPS - 1:

                    @pl.when(q > 1)
                    def _():
                        compute(last, (T + t) // 2)

                if t == 1:

                    @pl.when(q > 1)
                    def _():
                        compute(last, GROUPS - 1)
                        finish_chunk(last)

                if t == 2:
                    compute(q, 0)
                if t > LAG and t % 2 and t // 2 < GROUPS - 1:
                    compute(q, t // 2)
                if t == 4:

                    @pl.when(q == 0)
                    def _():
                        build(2)

                    @pl.when(q == 1)
                    def _():
                        build(3)

                if t == 6:

                    @pl.when(q == 0)
                    def _():
                        for group in range(4, GROUPS):
                            build(group)

                    @pl.when(q == 1)
                    def _():
                        receive_state()

                    @pl.when(q > 1)
                    def _():
                        receive_coupled(last)

                if t == T - 1:

                    @pl.when(q == 0)
                    def _():
                        loads[2].wait()
                        loads[3].wait()
                        kinetic(range(0, 6))

                    @pl.when(q == 1)
                    def _():
                        kinetic(range(6, 12))

    steps = Q * T
    ring_arrived(*chunk_round(steps - 3))
    sib_arrived(*chunk_round(steps - 4))
    ring_arrived(*chunk_round(steps - 2))
    sib_arrived(*chunk_round(steps - 3))
    if T % 2:
        compute(Q - 2, GROUPS - 2)
        compute(Q - 1, GROUPS - 2)
    sib_arrived(*chunk_round(steps - 2))
    compute(Q - 2, GROUPS - 1)
    finish_chunk(Q - 2)
    ring_arrived(*chunk_round(steps - 1))
    sib_arrived(*chunk_round(steps - 1))
    compute(Q - 1, GROUPS - 1)
    finish_chunk(Q - 1)
    receive_coupled(Q - 2)
    receive_coupled(Q - 1)

    def parts(q):
        re = pl.ds(q * 64, 32)
        im = pl.ds(q * 64 + 32, 32)
        return snat[re, :], snat[im, :], app[re, :], app[im, :]

    def fold(x):
        return jnp.sum(x, axis=0, keepdims=True)

    sums = [jnp.zeros((1, R), F32) for _ in range(3)]
    for q in range(Q):
        sre, sim, are, aim = parts(q)
        sums[0] += fold(sre * aim - sim * are)
        sums[1] -= fold(sre * are + sim * aim)
        sums[2] += fold(sre * sre + sim * sim)
    cross_re, cross_im, self_sq = (jnp.sum(x, axis=1, keepdims=True) for x in sums)

    def ratio(x, y):
        return jnp.where(y > 0.0, x / jnp.where(y > 0.0, y, 1.0), 0.0)

    own_re, own_im = ratio(cross_re, self_sq), ratio(cross_im, self_sq)
    left = jnp.zeros((1, R), F32)
    for q in range(Q):
        sre, sim, are, aim = parts(q)
        ore = aim - (own_re * sre - own_im * sim)
        oim = -are - (own_re * sim + own_im * sre)
        left += fold(ore * ore + oim * oim)
    left = jnp.sum(left, axis=1, keepdims=True)
    for i, value in enumerate((cross_re, cross_im, self_sq, left)):
        part[0, i : i + 1, :] = jnp.broadcast_to(value, (1, LANES))

    def scalar_copy(stage_, k):
        return pltpu.make_async_remote_copy(
            src_ref=part.at[stage_],
            dst_ref=gath.at[stage_, (me, rad)[stage_]],
            send_sem=sc_send.at[stage_, k],
            recv_sem=sc_recv.at[stage_, k],
            device_id=(chan_peer, rad_peer)[stage_](k),
            device_id_type=MESH,
        )

    def merge(stage_):
        for k in range(1, DEV):
            scalar_copy(stage_, k).start()
        gath[stage_, (me, rad)[stage_]] = part[stage_]
        for k in range(1, DEV):
            scalar_copy(stage_, k).wait_recv()
        rows = [[gath[stage_, j, i : i + 1, :] for j in range(DEV)] for i in range(4)]
        add = lambda xs: functools.reduce(lambda x, y: x + y, xs)
        cre, cim, sq = add(rows[0]), add(rows[1]), add(rows[2])
        pre, pim = ratio(cre, sq), ratio(cim, sq)
        rest = add(rows[3])
        for j in range(DEV):
            dre = pre - ratio(rows[0][j], rows[2][j])
            dim = pim - ratio(rows[1][j], rows[2][j])
            rest = rest + (dre * dre + dim * dim) * rows[2][j]
        return cre, cim, sq, rest, pre, pim

    merged = merge(0)
    for i in range(4):
        part[1, i : i + 1, :] = merged[i]
    _, _, _, rest, pre, pim = merge(1)
    rms = jnp.sqrt(rest / (2.0 * C * B * R) + 1e-06)
    place = lax.broadcasted_iota(jnp.int32, (1, 3), 1)
    coef_ref[...] = jnp.where(
        place == 0, pre[:, 0:3], jnp.where(place == 1, pim[:, 0:3], rms[:, 0:3])
    )
    pre1, pim1 = pre[:, 0:1], pim[:, 0:1]
    for q in range(Q):
        for i in range(4):
            re = slice(q * 64 + i * 8, q * 64 + i * 8 + 8)
            im = slice(q * 64 + 32 + i * 8, q * 64 + 32 + i * 8 + 8)
            sre, sim, are, aim = snat[re, :], snat[im, :], app[re, :], app[im, :]
            ore = aim - (pre1 * sre - pim1 * sim)
            oim = -are - (pre1 * sim + pim1 * sre)
            for tile in range(R // LANES):
                cols = slice(tile * LANES, tile * LANES + LANES)
                rows = tile * 256 + 4 * q + i
                rows_of[pl.ds(rows, 8, stride=2 * B), :] = ore[:, cols]
                rows_of[pl.ds(rows + B, 8, stride=2 * B), :] = oim[:, cols]
    for tile in range(R // LANES):
        out_ref[:, tile * LANES : tile * LANES + LANES] = rows_of[tile * 256 : tile * 256 + 256, :]

    for k in range(1, DEV):
        live_copy(k).wait_send()
        state_copy(k).wait_send()
        scalar_copy(0, k).wait_send()
        scalar_copy(1, k).wait_send()

    @pl.loop(0, Q)
    def _(q):
        sibx_copy(q).wait_send()
        for t in range(T):
            for way in range(2):
                ring_copy(q, t, way).wait_send()
            sib_copy(q, t).wait_send()
        for k in range(1, DEV):
            coupled_copy(q, k).wait_send()


def per_device(
    state, coupling, fetch_group, live_slots, radius_one, radius_two, kinetic_diag, kinetic_link
):
    vmem = pl.BlockSpec(memory_space=pltpu.VMEM)
    smem = pl.BlockSpec(memory_space=pltpu.SMEM)
    hbm = pl.BlockSpec(memory_space=pl.ANY)
    dma = pltpu.SemaphoreType.DMA
    rows_n = -(-4 * T // 8) * 8
    out, coef, flag = pl.pallas_call(
        kernel,
        out_shape=(
            jax.ShapeDtypeStruct((8 * 2 * B, R), F32),
            jax.ShapeDtypeStruct((1, 3), F32),
            jax.ShapeDtypeStruct((1,), jnp.int32),
        ),
        in_specs=[hbm, hbm, smem, smem, smem, vmem, hbm, hbm],
        out_specs=(vmem, vmem, smem),
        scratch_shapes=[
            pltpu.VMEM((2 * B * PTS, 128), F32),
            pltpu.VMEM((4 * 16 * 4 * GS, GS), F32),
            pltpu.VMEM((12, 128, 128), F32),
            pltpu.VMEM((11, 128, 128), F32),
            pltpu.VMEM((2, Q, 128, CELLS), F32),
            pltpu.VMEM((Q, T * 4 * GS, CELLS), F32),
            pltpu.VMEM((2, Q, T, GS, CELLS), F32),
            pltpu.VMEM((512, 512), BF16),
            pltpu.VMEM((512, 512), BF16),
            pltpu.VMEM((GROUPS, 512, 256), BF16),
            pltpu.VMEM((GROUPS, 512, 256), BF16),
            pltpu.VMEM((Q, 4, 8, CELLS), F32),
            pltpu.VMEM((2, 512, CELLS), F32),
            pltpu.VMEM((Q, 128, CELLS), F32),
            pltpu.VMEM((DEV, Q, 8, CELLS), F32),
            pltpu.VMEM((Q, DEV, 8, CELLS), F32),
            pltpu.VMEM((256, R), F32),
            pltpu.VMEM((256, R), F32),
            pltpu.VMEM((R // LANES * 256, LANES), F32),
            pltpu.VMEM((2, 8, LANES), F32),
            pltpu.VMEM((2, DEV, 8, LANES), F32),
            pltpu.VMEM((8, LANES), jnp.int32),
            pltpu.VMEM((DEV, 8, LANES), jnp.int32),
            pltpu.VMEM((rows_n, LANES), jnp.int32),
            pltpu.VMEM((rows_n, LANES), jnp.int32),
            pltpu.VMEM((rows_n, LANES), jnp.int32),
            pltpu.VMEM((8 + rows_n, LANES), jnp.int32),
            dma((4,)),
            dma((DEV,)),
            dma((DEV,)),
            dma((2, Q, T)),
            dma((2, Q, T)),
            dma((Q, T)),
            dma((Q, T)),
            dma((Q,)),
            dma((Q,)),
            dma((DEV,)),
            dma((DEV,)),
            dma((Q, DEV)),
            dma((Q, DEV)),
            dma((2, DEV)),
            dma((2, DEV)),
        ],
        compiler_params=pltpu.CompilerParams(
            collective_id=0, has_side_effects=True, vmem_limit_bytes=61 << 20
        ),
    )(
        state.transpose(1, 2, 3, 0).reshape(2 * B * PTS, 128),
        coupling.reshape(4 * 16 * 4 * GS, GS),
        fetch_group,
        live_slots,
        radius_one,
        radius_two.reshape(1, PTS),
        kinetic_diag,
        kinetic_link,
    )
    return lax.cond(
        flag[0] > 0,
        static_program,
        lambda *_: (out.reshape(8, 2, B, R), coef.reshape(3)),
        state,
        coupling,
        fetch_group,
        live_slots,
        radius_one,
        radius_two,
        kinetic_diag,
        kinetic_link,
    )


def solution(mesh):
    placed = (
        P("chan", None, None, "rad"),
        P("chan", None, None, None, None),
        P(),
        P("chan"),
        P(),
        P("rad"),
        P(),
        P(),
    )
    return jax.shard_map(
        per_device,
        mesh=mesh,
        in_specs=placed,
        out_specs=(P(("chan", "rad"), None, None, None), P()),
        check_vma=False,
    )
```

```python
import functools

import jax
import jax.numpy as jnp
from jax import lax
from jax.experimental import pallas as pl
from jax.experimental.pallas import tpu as pltpu
from jax.sharding import PartitionSpec as P

MESH = pl.DeviceIdType.MESH
F32 = jnp.float32
BF16 = jnp.bfloat16

C = 2048
R = 1536
B = 16
DEV = 16
Q = 4
CELLS = 768
GS = 32
T = 9
GROUPS = 1 + (T + 1) // 2
LAG = 2
OCTETS = 16
STATIC_T = 12
STATIC_GROUPS = 1 + STATIC_T // 2
LANES = 128
PTS = 96


def split(x):
    high = x.astype(BF16)
    return high, (x - high.astype(F32)).astype(BF16)


def pack4(a, b, c, d):
    return (
        jnp.concatenate([a, d[:, 0:32]], axis=1),
        jnp.concatenate([b, d[:, 32:64]], axis=1),
        jnp.concatenate([c, d[:, 64:96]], axis=1),
    )


def unpack4(t0, t1, t2):
    last = jnp.concatenate([t0[:, 96:128], t1[:, 96:128], t2[:, 96:128]], axis=1)
    return t0[:, 0:96], t1[:, 0:96], t2[:, 0:96], last


def static_kernel(
    state_ref,
    coup_ref,
    fetch_ref,
    live_ref,
    r1_ref,
    r2_ref,
    diag_ref,
    link_ref,
    out_ref,
    coef_ref,
    xp,
    sibx,
    pool,
    stage,
    wh,
    wl,
    kern,
    acc,
    cpl,
    srecv,
    crecv,
    snat,
    app,
    rows_of,
    part,
    gath,
    ring_send,
    ring_recv,
    sib_send,
    sib_recv,
    sx_send,
    sx_recv,
    st_send,
    st_recv,
    cp_send,
    cp_recv,
    sc_send,
    sc_recv,
):
    me = lax.axis_index("chan")
    rad = lax.axis_index("rad")
    core = lax.rem(me, 2)
    sib = me + 1 - 2 * core
    up = (lax.rem(me + 2, DEV), rad)
    down = (lax.rem(me + DEV - 2, DEV), rad)
    sibling = (sib, rad)

    def chan_peer(k):
        return (lax.rem(me + k, DEV), rad)

    def rad_peer(k):
        return (me, lax.rem(rad + k, DEV))

    barrier = pltpu.get_barrier_semaphore()
    for k in range(1, DEV):
        pl.semaphore_signal(barrier, inc=1, device_id=chan_peer(k), device_id_type=MESH)
        pl.semaphore_signal(barrier, inc=1, device_id=rad_peer(k), device_id_type=MESH)

    for q in range(Q):
        for plane in range(2):
            rows = [
                state_ref[pl.ds(plane * B + 4 * q + i, 128, stride=2 * B), :]
                for i in range(4)
            ]
            for i, tile in enumerate(pack4(*rows)):
                at = (plane * 3 + i) * LANES
                xp[q, :, at : at + LANES] = tile

    pl.semaphore_wait(barrier, 2 * (DEV - 1))

    def slot(t, side, way):
        return (t * 4 + side * 2 + way) * GS

    def ring_copy(q, t, way, src):
        return pltpu.make_async_remote_copy(
            src_ref=src,
            dst_ref=pool.at[q, pl.ds(slot(t, 0, way), GS), :],
            send_sem=ring_send.at[way, q, t],
            recv_sem=ring_recv.at[way, q, t],
            device_id=(up, down)[way],
            device_id_type=MESH,
        )

    def ring_src(q, t, way):
        if t < 4:
            return xp.at[q, pl.ds(GS * t, GS), :]
        if t < 8:
            return pool.at[q, pl.ds(slot(t - 4, 0, way), GS), :]
        if t < 11:
            return stage.at[q, way * 3 + t - 8]
        return pool.at[q, pl.ds(slot(10, 0, way), GS), :]

    def fetched(dest, source):
        return fetch_ref[dest, source]

    def wrap(x):
        return lax.rem(x + 2 * DEV, DEV)

    picks = []
    for way in range(2):
        sign = 1 if way == 0 else -1
        source = wrap(me - 4 * sign)
        near = wrap(me - core + 2 * sign)
        far = wrap(me - core + 4 * sign)
        far_core = core if way == 0 else 1 - core
        picks.append(
            [
                fetched(near, source),
                fetched(near + 1, source),
                fetched(far + far_core, source),
            ]
        )

    def ring_start(q, t):
        for way in range(2):
            if 8 <= t < 11:
                pick = picks[way][t - 8]
                chosen = pool[q, pl.ds(slot(4, 0, way), GS), :]
                for h in range(1, 4):
                    chosen = jnp.where(
                        pick == h, pool[q, pl.ds(slot(4 + h, 0, way), GS), :], chosen
                    )
                stage[q, way * 3 + t - 8] = chosen
            ring_copy(q, t, way, ring_src(q, t, way)).start()

    def sib_copy(q, t):
        return pltpu.make_async_remote_copy(
            src_ref=pool.at[q, pl.ds(slot(t, 0, 0), 2 * GS), :],
            dst_ref=pool.at[q, pl.ds(slot(t, 1, 0), 2 * GS), :],
            send_sem=sib_send.at[q, t],
            recv_sem=sib_recv.at[q, t],
            device_id=sibling,
            device_id_type=MESH,
        )

    def arrived(q, t):
        for way in range(2):
            ring_copy(q, t, way, ring_src(q, t, way)).wait_recv()
        sib_copy(q, t).start()

    def sib_arrived(q, t):
        sib_copy(q, t).wait_recv()

    sibx_copy = pltpu.make_async_remote_copy(
        src_ref=xp,
        dst_ref=sibx,
        send_sem=sx_send.at[0],
        recv_sem=sx_recv.at[0],
        device_id=sibling,
        device_id_type=MESH,
    )

    def state_copy(k):
        return pltpu.make_async_remote_copy(
            src_ref=xp.at[:, pl.ds(8 * lax.rem(rad + k, DEV), 8), :],
            dst_ref=srecv.at[rad],
            send_sem=st_send.at[k],
            recv_sem=st_recv.at[k],
            device_id=rad_peer(k),
            device_id_type=MESH,
        )

    def coupled_copy(q, k):
        return pltpu.make_async_remote_copy(
            src_ref=cpl.at[q, pl.ds(8 * lax.rem(rad + k, DEV), 8), :],
            dst_ref=crecv.at[q, rad],
            send_sem=cp_send.at[q, k],
            recv_sem=cp_recv.at[q, k],
            device_id=rad_peer(k),
            device_id_type=MESH,
        )

    ring_start(0, 0)
    ring_start(0, 1)
    sibx_copy.start()
    for k in range(1, DEV):
        state_copy(k).start()
    ring_start(0, 2)
    ring_start(0, 3)
    srecv[rad] = xp[:, pl.ds(pl.multiple_of(8 * rad, 8), 8), :]

    row = jnp.broadcast_to(r2_ref[0:1, :], (8, PTS))
    tails = pack4(row, row, row, row)
    lane = lax.broadcasted_iota(jnp.int32, (8, LANES), 1)
    for q in range(Q):
        for i in range(3):
            one = jnp.where(lane < PTS, r1_ref[4 * q + i], r1_ref[4 * q + 3])
            nearer = jnp.minimum(one, tails[i])
            farther = jnp.maximum(one, tails[i])
            top = jnp.ones_like(nearer)
            bottom = farther
            for order in range(4):
                value = top / bottom
                for plane in range(2):
                    at = (plane * 3 + i) * LANES
                    kern[q, order, :, at : at + LANES] = value
                top = top * nearer
                bottom = bottom * farther

    def put_weight(group, place, k, take):
        for g in range(4):
            on = jnp.where(live_ref[g] > k, take, 0.0)
            for order in range(4):
                start = ((g * 16 + k) * 4 + order) * GS
                block = coup_ref[pl.ds(pl.multiple_of(start, GS), GS), :] * on
                high, low = split(block)
                rows = slice(order * 128 + g * GS, order * 128 + g * GS + GS)
                cols = slice(place * GS, place * GS + GS)
                wh[group, rows, cols] = high
                wl[group, rows, cols] = low

    def one_if(condition):
        return jnp.where(condition, 1.0, 0.0)

    def build(group):
        if group == 0:
            for h in range(4):
                put_weight(0, h, 0, one_if(fetched(me, me) == h))
                put_weight(
                    0, 4 + h, wrap(sib - me), one_if(fetched(me, sib) == h)
                )
            return
        for t in (2 * group - 2, 2 * group - 1):
            dist = 1 if t < 4 else 2 if t < 8 else 3 if t < 11 else 4
            for side in range(2):
                for way in range(2):
                    home = me if side == 0 else sib
                    source = wrap(home - 2 * dist if way == 0 else home + 2 * dist)
                    if t < 8:
                        take = one_if(fetched(me, source) == t % 4)
                    elif t < 10:
                        take = one_if(core == t - 8)
                    elif t == 10:
                        take = 0.0
                    else:
                        take = float(side == way)
                    place = (t % 2) * 4 + side * 2 + way
                    put_weight(group, place, wrap(source - me), take)

    def multiply(q, group, read):
        @pl.loop(0, 3)
        def _(j):
            at = pl.multiple_of(j * 256, 256)
            xh, xl = split(read(at))
            dot = functools.partial(jnp.dot, preferred_element_type=F32)
            total = dot(wh[group], xh) + dot(wl[group], xh) + dot(wh[group], xl)
            if group == 0:
                acc[:, pl.ds(at, 256)] = total
            else:
                acc[:, pl.ds(at, 256)] += total

    def compute(q, group):
        if group == 0:
            multiply(
                q,
                0,
                lambda at: jnp.concatenate(
                    [xp[q, :, pl.ds(at, 256)], sibx[q, :, pl.ds(at, 256)]], axis=0
                ),
            )
        else:
            multiply(
                q,
                group,
                lambda at: pool[q, pl.ds(256 * (group - 1), 256), pl.ds(at, 256)],
            )

    def finish_chunk(q):
        for tile in range(6):
            cols = slice(tile * LANES, tile * LANES + LANES)
            total = jnp.zeros((128, LANES), F32)
            for order in range(4):
                factor = jnp.broadcast_to(kern[q, order, 0:1, cols], (128, LANES))
                total = total + acc[order * 128 : order * 128 + 128, cols] * factor
            cpl[q, :, cols] = total
        for k in range(1, DEV):
            coupled_copy(q, k).start()
        crecv[q, rad] = cpl[q, pl.ds(pl.multiple_of(8 * rad, 8), 8), :]

    def natural(piece):
        out = []
        for plane in range(2):
            cols = [slice((plane * 3 + i) * LANES, (plane * 3 + i + 1) * LANES) for i in range(3)]
            parts = [unpack4(*(piece(s, c) for c in cols)) for s in range(4)]
            for i in range(4):
                out.append(jnp.concatenate([p[i] for p in parts], axis=1))
        return out

    def kinetic_all():
        for k in range(1, DEV):
            state_copy(k).wait_recv()
        for q in range(Q):
            for quad in range(4):
                for i, value in enumerate(
                    natural(lambda s, c: srecv[4 * quad + s, q, :, c])
                ):
                    rows = slice(q * 64 + i * 8, q * 64 + i * 8 + 8)
                    snat[rows, 384 * quad : 384 * quad + 384] = value
        high = functools.partial(
            lax.dot_general, precision=lax.Precision.HIGHEST, preferred_element_type=F32
        )
        same = (((1,), (1,)), ((), ()))
        flip = (((1,), (0,)), ((), ()))
        for e in range(12):
            cols = [slice(128 * x, 128 * x + 128) for x in (e - 1, e, e + 1)]
            value = high(snat[:, cols[1]], diag_ref[e], same)
            if e > 0:
                value = value + high(snat[:, cols[0]], link_ref[e - 1], same)
            if e < 11:
                value = value + high(snat[:, cols[2]], link_ref[e], flip)
            app[:, cols[1]] = value

    def receive_coupled(q):
        for k in range(1, DEV):
            coupled_copy(q, k).wait_recv()
        for quad in range(4):
            for i, value in enumerate(
                natural(lambda s, c: crecv[q, 4 * quad + s, :, c])
            ):
                rows = pl.ds(pl.multiple_of(q * 64 + i * 8, 8), 8)
                cols = slice(384 * quad, 384 * quad + 384)
                app[rows, cols] += value

    def tail(q):
        arrived(q, 11)
        sib_arrived(q, 10)
        sib_arrived(q, 11)
        compute(q, 6)
        finish_chunk(q)

    build(0)
    sibx_copy.wait_recv()

    @pl.loop(0, Q)
    def _(q):
        nxt = q + 1
        more = q < Q - 1
        arrived(q, 0)
        ring_start(q, 4)
        arrived(q, 1)
        ring_start(q, 5)

        @pl.when(q > 0)
        def _():
            tail(q - 1)

        arrived(q, 2)
        ring_start(q, 6)
        arrived(q, 3)
        ring_start(q, 7)

        @pl.when(q == 0)
        def _():
            for group in range(1, 4):
                build(group)

        compute(q, 0)

        @pl.when(more)
        def _():
            ring_start(nxt, 0)
            ring_start(nxt, 1)

        sib_arrived(q, 0)
        sib_arrived(q, 1)
        compute(q, 1)
        for t in range(4, 8):
            arrived(q, t)
        for t in range(8, 11):
            ring_start(q, t)

        @pl.when(more)
        def _():
            ring_start(nxt, 2)
            ring_start(nxt, 3)

        @pl.when(q == 0)
        def _():
            for group in range(4, STATIC_GROUPS):
                build(group)

        sib_arrived(q, 2)
        sib_arrived(q, 3)
        compute(q, 2)
        for t in range(8, 11):
            arrived(q, t)
        ring_start(q, 11)
        for t in range(4, 10):
            sib_arrived(q, t)
        for group in range(3, 6):
            compute(q, group)

        @pl.when(q == 0)
        def _():
            kinetic_all()

        @pl.when(q > 0)
        def _():
            receive_coupled(q - 1)

    tail(Q - 1)
    receive_coupled(Q - 1)

    def parts(q):
        re = pl.ds(q * 64, 32)
        im = pl.ds(q * 64 + 32, 32)
        return snat[re, :], snat[im, :], app[re, :], app[im, :]

    def fold(x):
        return jnp.sum(x, axis=0, keepdims=True)

    sums = [jnp.zeros((1, R), F32) for _ in range(3)]
    for q in range(Q):
        sre, sim, are, aim = parts(q)
        sums[0] += fold(sre * aim - sim * are)
        sums[1] -= fold(sre * are + sim * aim)
        sums[2] += fold(sre * sre + sim * sim)
    cross_re, cross_im, self_sq = (jnp.sum(x, axis=1, keepdims=True) for x in sums)

    def ratio(x, y):
        return jnp.where(y > 0.0, x / jnp.where(y > 0.0, y, 1.0), 0.0)

    own_re, own_im = ratio(cross_re, self_sq), ratio(cross_im, self_sq)
    left = jnp.zeros((1, R), F32)
    for q in range(Q):
        sre, sim, are, aim = parts(q)
        ore = aim - (own_re * sre - own_im * sim)
        oim = -are - (own_re * sim + own_im * sre)
        left += fold(ore * ore + oim * oim)
    left = jnp.sum(left, axis=1, keepdims=True)
    for i, value in enumerate((cross_re, cross_im, self_sq, left)):
        part[0, i : i + 1, :] = jnp.broadcast_to(value, (1, LANES))

    def scalar_copy(stage_, k):
        return pltpu.make_async_remote_copy(
            src_ref=part.at[stage_],
            dst_ref=gath.at[stage_, (me, rad)[stage_]],
            send_sem=sc_send.at[stage_, k],
            recv_sem=sc_recv.at[stage_, k],
            device_id=(chan_peer, rad_peer)[stage_](k),
            device_id_type=MESH,
        )

    def merge(stage_):
        for k in range(1, DEV):
            scalar_copy(stage_, k).start()
        gath[stage_, (me, rad)[stage_]] = part[stage_]
        for k in range(1, DEV):
            scalar_copy(stage_, k).wait_recv()
        rows = [[gath[stage_, j, i : i + 1, :] for j in range(DEV)] for i in range(4)]
        add = lambda xs: functools.reduce(lambda x, y: x + y, xs)
        cre, cim, sq = add(rows[0]), add(rows[1]), add(rows[2])
        pre, pim = ratio(cre, sq), ratio(cim, sq)
        rest = add(rows[3])
        for j in range(DEV):
            dre = pre - ratio(rows[0][j], rows[2][j])
            dim = pim - ratio(rows[1][j], rows[2][j])
            rest = rest + (dre * dre + dim * dim) * rows[2][j]
        return cre, cim, sq, rest, pre, pim

    merged = merge(0)
    for i in range(4):
        part[1, i : i + 1, :] = merged[i]
    _, _, _, rest, pre, pim = merge(1)
    rms = jnp.sqrt(rest / (2.0 * C * B * R) + 1e-06)
    coef_ref[0:1, :] = pre
    coef_ref[1:2, :] = pim
    coef_ref[2:3, :] = rms
    pre1, pim1 = pre[:, 0:1], pim[:, 0:1]
    for q in range(Q):
        for i in range(4):
            re = slice(q * 64 + i * 8, q * 64 + i * 8 + 8)
            im = slice(q * 64 + 32 + i * 8, q * 64 + 32 + i * 8 + 8)
            sre, sim, are, aim = snat[re, :], snat[im, :], app[re, :], app[im, :]
            ore = aim - (pre1 * sre - pim1 * sim)
            oim = -are - (pre1 * sim + pim1 * sre)
            for tile in range(R // LANES):
                cols = slice(tile * LANES, tile * LANES + LANES)
                rows = tile * 256 + 4 * q + i
                rows_of[pl.ds(rows, 8, stride=2 * B), :] = ore[:, cols]
                rows_of[pl.ds(rows + B, 8, stride=2 * B), :] = oim[:, cols]
    for tile in range(R // LANES):
        out_ref[:, tile * LANES : tile * LANES + LANES] = rows_of[tile * 256 : tile * 256 + 256, :]

    sibx_copy.wait_send()
    for k in range(1, DEV):
        state_copy(k).wait_send()
        scalar_copy(0, k).wait_send()
        scalar_copy(1, k).wait_send()

    @pl.loop(0, Q)
    def _(q):
        for t in range(STATIC_T):
            for way in range(2):
                ring_copy(q, t, way, ring_src(q, t, way)).wait_send()
            sib_copy(q, t).wait_send()
        for k in range(1, DEV):
            coupled_copy(q, k).wait_send()


def static_program(
    state, coupling, fetch_group, live_slots, radius_one, radius_two, kinetic_diag, kinetic_link
):
    vmem = pl.BlockSpec(memory_space=pltpu.VMEM)
    smem = pl.BlockSpec(memory_space=pltpu.SMEM)
    dma = pltpu.SemaphoreType.DMA
    out, coef = pl.pallas_call(
        static_kernel,
        out_shape=(
            jax.ShapeDtypeStruct((8 * 2 * B, R), F32),
            jax.ShapeDtypeStruct((8, LANES), F32),
        ),
        in_specs=[vmem, vmem, smem, smem, smem, vmem, vmem, vmem],
        out_specs=(vmem, vmem),
        scratch_shapes=[
            pltpu.VMEM((Q, 128, CELLS), F32),
            pltpu.VMEM((Q, 128, CELLS), F32),
            pltpu.VMEM((Q, STATIC_T * 4 * GS, CELLS), F32),
            pltpu.VMEM((Q, 6, GS, CELLS), F32),
            pltpu.VMEM((STATIC_GROUPS, 512, 256), BF16),
            pltpu.VMEM((STATIC_GROUPS, 512, 256), BF16),
            pltpu.VMEM((Q, 4, 8, CELLS), F32),
            pltpu.VMEM((512, CELLS), F32),
            pltpu.VMEM((Q, 128, CELLS), F32),
            pltpu.VMEM((DEV, Q, 8, CELLS), F32),
            pltpu.VMEM((Q, DEV, 8, CELLS), F32),
            pltpu.VMEM((256, R), F32),
            pltpu.VMEM((256, R), F32),
            pltpu.VMEM((R // LANES * 256, LANES), F32),
            pltpu.VMEM((2, 8, LANES), F32),
            pltpu.VMEM((2, DEV, 8, LANES), F32),
            dma((2, Q, STATIC_T)),
            dma((2, Q, STATIC_T)),
            dma((Q, STATIC_T)),
            dma((Q, STATIC_T)),
            dma((1,)),
            dma((1,)),
            dma((DEV,)),
            dma((DEV,)),
            dma((Q, DEV)),
            dma((Q, DEV)),
            dma((2, DEV)),
            dma((2, DEV)),
        ],
        compiler_params=pltpu.CompilerParams(
            collective_id=1, has_side_effects=True, vmem_limit_bytes=61 << 20
        ),
    )(
        state.reshape(128 * 2 * B, PTS),
        coupling.reshape(4 * 16 * 4 * GS, GS),
        fetch_group,
        live_slots,
        radius_one,
        radius_two.reshape(1, PTS),
        kinetic_diag,
        kinetic_link,
    )
    return out.reshape(8, 2, B, R), coef[0:3, 0]


def tie_up(v, dest_z, dest_core, source_core):
    index = dest_z * 4 + dest_core * 2 + source_core
    mixed = (((v * 5 + 3) * (index + 1) * (index + 7)) >> 3) & 1
    odd = (dest_core + source_core) & 1
    return jnp.where(
        v == 0,
        1 - odd,
        jnp.where(v == 1, odd, jnp.where(v == 2, 1 - source_core, jnp.where(v == 3, source_core, mixed))),
    )


def flat4(t0, t1, t2):
    return (
        t0[:, 0:96],
        jnp.concatenate([t0[:, 96:128], t1[:, 0:64]], axis=1),
        jnp.concatenate([t1[:, 64:128], t2[:, 0:32]], axis=1),
        t2[:, 32:128],
    )


def kernel(
    state_hbm,
    coup_hbm,
    fetch_ref,
    live_ref,
    r1_ref,
    r2_ref,
    diag_hbm,
    link_hbm,
    out_ref,
    coef_ref,
    flag_ref,
    state_v,
    coup_v,
    diag_v,
    link_v,
    xb,
    pool,
    stage,
    ch,
    cl,
    wh,
    wl,
    kern,
    acc,
    cpl,
    srecv,
    crecv,
    s_nat,
    k_nat,
    a_nat,
    kout,
    krecv,
    stat,
    part,
    gath,
    live_out,
    live_in,
    sim_key,
    sim_read,
    read_table,
    slot_table,
    load_sem,
    live_send,
    live_recv,
    ring_send,
    ring_recv,
    sib_send,
    sib_recv,
    sx_send,
    sx_recv,
    st_send,
    st_recv,
    cp_send,
    cp_recv,
    kn_send,
    kn_recv,
    sc_send,
    sc_recv,
):
    me = lax.axis_index("chan")
    rad = lax.axis_index("rad")
    core = lax.rem(me, 2)
    chip = me // 2
    sib = me + 1 - 2 * core
    up = (lax.rem(me + 2, DEV), rad)
    down = (lax.rem(me + DEV - 2, DEV), rad)
    sibling = (sib, rad)

    def chan_peer(k):
        return (lax.rem(me + k, DEV), rad)

    def rad_peer(k):
        return (me, lax.rem(rad + k, DEV))

    loads = [
        pltpu.make_async_copy(src, dst, load_sem.at[i])
        for i, (src, dst) in enumerate(
            ((state_hbm, state_v), (coup_hbm, coup_v), (diag_hbm, diag_v), (link_hbm, link_v))
        )
    ]
    for load in loads:
        load.start()
    barrier = pltpu.get_barrier_semaphore()
    for k in range(1, DEV):
        pl.semaphore_signal(barrier, inc=1, device_id=chan_peer(k), device_id_type=MESH)
        pl.semaphore_signal(barrier, inc=1, device_id=rad_peer(k), device_id_type=MESH)

    mine = jnp.maximum(
        jnp.maximum(live_ref[0], live_ref[1]), jnp.maximum(live_ref[2], live_ref[3])
    )
    live_out[...] = jnp.full((8, LANES), mine, jnp.int32)

    lane = lax.broadcasted_iota(jnp.int32, (8, LANES), 1)
    sub = lax.broadcasted_iota(jnp.int32, (8, LANES), 0)
    lane_z = lane & 7
    octet = lane >> 3
    sub_core = sub >> 2
    sub_block = sub & 3
    spots = [[(lane_z == z) & (sub_core == s) for s in range(2)] for z in range(8)]
    taken = {}
    for delta in range(1, 8):
        for dest_core in range(2):
            value = jnp.zeros((8, LANES), jnp.int32)
            for z in range(8):
                for s in range(2):
                    picked = fetch_ref[2 * ((z + delta) % 8) + dest_core, 2 * z + s]
                    value = jnp.where(spots[z][s], picked, value)
            taken[delta, dest_core] = value == sub_block

    def live_copy(k):
        return pltpu.make_async_remote_copy(
            src_ref=live_out,
            dst_ref=live_in.at[me],
            send_sem=live_send.at[k],
            recv_sem=live_recv.at[k],
            device_id=chan_peer(k),
            device_id_type=MESH,
        )

    def sibx_copy(q):
        return pltpu.make_async_remote_copy(
            src_ref=xb.at[core, q],
            dst_ref=xb.at[core, q],
            send_sem=sx_send.at[q],
            recv_sem=sx_recv.at[q],
            device_id=sibling,
            device_id_type=MESH,
        )

    def state_copy(k):
        return pltpu.make_async_remote_copy(
            src_ref=xb.at[core, :, pl.ds(8 * lax.rem(rad + k, DEV), 8), :],
            dst_ref=srecv.at[rad],
            send_sem=st_send.at[k],
            recv_sem=st_recv.at[k],
            device_id=rad_peer(k),
            device_id_type=MESH,
        )

    def coupled_copy(q, k):
        return pltpu.make_async_remote_copy(
            src_ref=cpl.at[q, pl.ds(8 * lax.rem(rad + k, DEV), 8), :],
            dst_ref=crecv.at[q, rad],
            send_sem=cp_send.at[q, k],
            recv_sem=cp_recv.at[q, k],
            device_id=rad_peer(k),
            device_id_type=MESH,
        )

    def slot(t, side, way):
        return pl.multiple_of((t * 4 + side * 2 + way) * GS, GS)

    def ring_copy(q, t, way):
        return pltpu.make_async_remote_copy(
            src_ref=stage.at[way, q, t],
            dst_ref=pool.at[q, pl.ds(slot(t, core, way), GS), :],
            send_sem=ring_send.at[way, q, t],
            recv_sem=ring_recv.at[way, q, t],
            device_id=(up, down)[way],
            device_id_type=MESH,
        )

    def sib_copy(q, t):
        return pltpu.make_async_remote_copy(
            src_ref=pool.at[q, pl.ds(slot(t, core, 0), 2 * GS), :],
            dst_ref=pool.at[q, pl.ds(slot(t, core, 0), 2 * GS), :],
            send_sem=sib_send.at[q, t],
            recv_sem=sib_recv.at[q, t],
            device_id=sibling,
            device_id_type=MESH,
        )

    pl.semaphore_wait(barrier, 2 * (DEV - 1))
    for k in range(1, DEV):
        live_copy(k).start()
    live_in[me] = live_out[...]

    loads[0].wait()
    for q in range(Q):
        for plane in range(2):
            rows = slice(plane * B * PTS + 384 * q, plane * B * PTS + 384 * q + 384)
            xb[core, q, :, plane * 384 : plane * 384 + 384] = jnp.transpose(state_v[rows, :])
        sibx_copy(q).start()
    for k in range(1, DEV):
        state_copy(k).start()
    srecv[rad] = xb[core, :, pl.ds(pl.multiple_of(8 * rad, 8), 8), :]

    for k in range(1, DEV):
        live_copy(k).wait_recv()
    most = []
    for dest_core in range(2):
        value = live_in[dest_core]
        for z in range(1, 8):
            value = jnp.where(lane_z == z, live_in[2 * z + dest_core], value)
        most.append(value)

    def turn(x, shift):
        shift = shift % 8
        if shift == 0:
            return x
        return jnp.where(
            lane_z >= shift,
            pltpu.roll(x, shift, 1),
            pltpu.roll(x, LANES - 8 + shift, 1),
        )

    reach = []
    for way in range(2):
        value = jnp.zeros((8, LANES), jnp.int32)
        for dist in range(1, 5):
            delta = dist if way == 0 else 8 - dist
            for dest_core in range(2):
                k = ((2 * dist if way else -2 * dist) + sub_core - dest_core) & 15
                need = taken[delta, dest_core] & (
                    k < pltpu.roll(most[dest_core], LANES - delta, 1)
                )
                if dist == 4:
                    upward = tie_up(octet, (lane_z + 4) & 7, dest_core, sub_core)
                    need = need & (upward == 1 - way)
                value = jnp.where(need, dist, value)
        reach.append(value)

    waiting, ready, where_from = [], [], []
    for way in range(2):
        here = [turn(reach[way], j if way == 0 else -j) for j in range(4)]
        waiting.append(
            [jnp.where(r > j, (r - j) * 32 + j * 8 + sub, 0) for j, r in enumerate(here)]
        )
        ready.append([jnp.full((8, LANES), 0 if j == 0 else 99, jnp.int32) for j in range(4)])
        where_from.append([sub for _ in range(4)])

    def peak(x):
        for shift in (4, 2, 1):
            x = jnp.maximum(x, pltpu.roll(x, shift, 0))
        return x

    sim_key[...] = jnp.zeros(sim_key.shape, jnp.int32)
    sim_read[...] = jnp.zeros(sim_read.shape, jnp.int32)
    for t in range(T):
        for way in range(2):
            wait, soon, source = waiting[way], ready[way], where_from[way]
            sent = [jnp.zeros((8, LANES), jnp.int32) for _ in range(4)]
            for side in range(2):
                open_ = [
                    jnp.where((soon[j] <= t) & (sent[j] == 0), wait[j], 0) for j in range(4)
                ]
                top = peak(functools.reduce(jnp.maximum, open_))
                chosen = [(open_[j] == top) & (top > 0) for j in range(4)]
                code = peak(
                    functools.reduce(
                        jnp.maximum,
                        [jnp.where(chosen[j], source[j] + 1, 0) for j in range(4)],
                    )
                )
                row = t * 4 + side * 2 + way
                sim_key[row : row + 1, :] = top[0:1, :]
                sim_read[row : row + 1, :] = code[0:1, :]
                sent = [jnp.where(chosen[j], side + 1, sent[j]) for j in range(4)]
            waiting[way] = [jnp.where(sent[j] > 0, 0, wait[j]) for j in range(4)]
            for j in range(3):
                came = turn(sent[j], 1 if way == 0 else -1)
                soon[j + 1] = jnp.where(came > 0, t + LAG, soon[j + 1])
                source[j + 1] = jnp.where(came > 0, 8 + 2 * t - 1 + came, source[j + 1])

    left = peak(functools.reduce(jnp.maximum, waiting[0] + waiting[1]))
    for shift in (4, 2, 1):
        left = jnp.maximum(left, turn(left, shift))
    routing = jnp.min(
        jnp.where(left > 0, 99.0, octet.astype(F32)), axis=1, keepdims=True
    )
    flag_ref[0] = jnp.where(jnp.max(routing) > 50.0, 1, 0)
    routing = jnp.where(routing > 50.0, 0.0, routing).astype(jnp.int32)[0:1, :]

    rows_n = sim_key.shape[0]
    wide = lax.broadcasted_iota(jnp.int32, (rows_n, LANES), 1)
    tall = lax.broadcasted_iota(jnp.int32, (rows_n, LANES), 0)

    def column(table, z):
        hit = wide == routing * 8 + z
        picked = jnp.where(hit, table.astype(F32), 0.0)
        return jnp.broadcast_to(
            jnp.sum(picked, axis=1, keepdims=True), (rows_n, LANES)
        ).astype(jnp.int32)

    read_table[...] = column(sim_read[...], chip)
    came_way = tall & 1
    key = column(
        sim_key[...], jnp.where(came_way == 0, (chip + 7) & 7, (chip + 1) & 7)
    )
    ident = key & 31
    dist = (ident >> 3) + 1
    from_core = (ident >> 2) & 1
    from_block = ident & 3
    k = (jnp.where(came_way == 0, -2 * dist, 2 * dist) + from_core - core) & 15
    fetched = jnp.zeros_like(k)
    for j in range(DEV):
        fetched = jnp.where(k == j, fetch_ref[me, lax.rem(me + j, DEV)], fetched)
    upward = tie_up(jnp.broadcast_to(routing, (rows_n, LANES)), chip, core, from_core)
    take = (key > 0) & (fetched == from_block) & (tall < 4 * T)
    take = take & ((dist < 4) | (upward == 1 - came_way))
    slot_table[8 : 8 + rows_n, :] = jnp.where(take, k, -1)
    own = jnp.where(
        sub_core == 0,
        fetch_ref[me, me - core],
        fetch_ref[me, me - core + 1],
    )
    slot_table[0:8, :] = jnp.where(own == sub_block, (sub_core - core) & 15, -1)

    def ring_start(q, t):
        for way in range(2):
            row = t * 4 + way
            code = jnp.where(
                jnp.full((1, LANES), core, jnp.int32) == 0,
                read_table[row : row + 1, :],
                read_table[row + 2 : row + 3, :],
            )
            code = jnp.broadcast_to(code, (GS, LANES))
            tiles = [slice(i * LANES, i * LANES + LANES) for i in range(6)]
            chosen = [xb[0, q, 0:GS, c] for c in tiles]
            for i in range(1, 8 + 2 * max(0, t - LAG + 1)):
                hit = code == i + 1
                for n, c in enumerate(tiles):
                    if i < 8:
                        rows = pl.ds((i % 4) * GS, GS)
                        block = xb[i // 4, q, rows, c]
                    else:
                        block = pool[q, pl.ds(slot((i - 8) // 2, i % 2, way), GS), c]
                    chosen[n] = jnp.where(hit, block, chosen[n])
            for n, c in enumerate(tiles):
                stage[way, q, t, :, c] = chosen[n]
            ring_copy(q, t, way).start()

    def ring_arrived(q, t):
        for way in range(2):
            ring_copy(q, t, way).wait_recv()
        sib_copy(q, t).start()

    def sib_arrived(q, t):
        sib_copy(q, t).wait_recv()

    def build_coupling():
        loads[1].wait()
        for g in range(4):
            for four in range(4):
                on = [
                    jnp.where(live_ref[g] > 4 * four + j, 1.0, 0.0) for j in range(4)
                ]
                for order in range(4):
                    block = jnp.concatenate(
                        [
                            coup_v[pl.ds(((g * 16 + 4 * four + j) * 4 + order) * GS, GS), :]
                            * on[j]
                            for j in range(4)
                        ],
                        axis=1,
                    )
                    high, low = split(block)
                    rows = slice(order * 128 + g * GS, order * 128 + g * GS + GS)
                    cols = slice(four * LANES, four * LANES + LANES)
                    ch[rows, cols] = high
                    cl[rows, cols] = low

    def build(group):
        width = 256 if group < GROUPS - 1 or T % 2 == 0 else 128
        depth = lax.broadcasted_iota(jnp.int32, (512, LANES), 0)
        across = lax.broadcasted_iota(jnp.int32, (1, LANES), 1)
        for half in range(width // 128):
            target = jnp.full((1, LANES), -1, jnp.int32)
            for p in range(4):
                row = 8 * group + 4 * half + p
                target = jnp.where(across >> 5 == p, slot_table[row : row + 1, :], target)
            target = target * GS + (across & 31)
            select = jnp.where(depth == target, 1.0, 0.0).astype(BF16)
            cols = slice(half * 128, half * 128 + 128)
            for src, dst in ((ch, wh), (cl, wl)):
                dst[group, :, cols] = jnp.dot(
                    src[...], select, preferred_element_type=F32
                ).astype(BF16)

    def compute(q, group):
        half = lax.rem(q, 2)
        width = 256 if group < GROUPS - 1 or T % 2 == 0 else 128

        @pl.loop(0, 3)
        def _(j):
            at = pl.multiple_of(j * 256, 256)
            if group == 0:
                x = jnp.concatenate(
                    [xb[0, q, :, pl.ds(at, 256)], xb[1, q, :, pl.ds(at, 256)]], axis=0
                )
            else:
                x = pool[q, pl.ds(256 * (group - 1), width), pl.ds(at, 256)]
            xh, xl = split(x)
            dot = functools.partial(jnp.dot, preferred_element_type=F32)
            gh, gl = wh[group, :, 0:width], wl[group, :, 0:width]
            total = dot(gh, xh) + dot(gl, xh) + dot(gh, xl)
            if group == 0:
                acc[half, :, pl.ds(at, 256)] = total
            else:
                acc[half, :, pl.ds(at, 256)] += total

    def build_kern():
        row = jnp.broadcast_to(r2_ref[0:1, :], (8, PTS))
        flat = jnp.concatenate([row] * 4, axis=1)
        point = lax.broadcasted_iota(jnp.int32, (8, 384), 1)
        for q in range(Q):
            one = jnp.where(
                point < PTS,
                r1_ref[4 * q],
                jnp.where(
                    point < 2 * PTS,
                    r1_ref[4 * q + 1],
                    jnp.where(point < 3 * PTS, r1_ref[4 * q + 2], r1_ref[4 * q + 3]),
                ),
            )
            nearer = jnp.minimum(one, flat)
            farther = jnp.maximum(one, flat)
            top = jnp.ones_like(nearer)
            bottom = farther
            for order in range(4):
                value = top / bottom
                kern[q, order, :, 0:384] = value
                kern[q, order, :, 384:768] = value
                top = top * nearer
                bottom = bottom * farther

    def fold_orders(q):
        half = lax.rem(q, 2)
        for tile in range(6):
            cols = slice(tile * LANES, tile * LANES + LANES)
            total = jnp.zeros((128, LANES), F32)
            for order in range(4):
                factor = jnp.broadcast_to(kern[q, order, 0:1, cols], (128, LANES))
                total = total + acc[half, order * 128 : order * 128 + 128, cols] * factor
            cpl[q, :, cols] = total

    def kinetic_copy(k):
        return pltpu.make_async_remote_copy(
            src_ref=kout.at[lax.rem(rad + k, DEV)],
            dst_ref=krecv.at[:, pl.ds(8 * rad, 8), :],
            send_sem=kn_send.at[k],
            recv_sem=kn_recv.at[k],
            device_id=rad_peer(k),
            device_id_type=MESH,
        )

    def fold(x):
        return jnp.sum(jnp.sum(x, axis=0, keepdims=True), axis=1, keepdims=True)

    def ratio(x, y):
        return jnp.where(y > 0.0, x / jnp.where(y > 0.0, y, 1.0), 0.0)

    def send_chunk(q):
        for tile in range(6):
            cols = slice(tile * LANES, tile * LANES + LANES)
            cpl[q, :, cols] += krecv[q, :, cols]
        for k in range(1, DEV):
            coupled_copy(q, k).start()
        crecv[q, rad] = cpl[q, pl.ds(pl.multiple_of(8 * rad, 8), 8), :]
        sre, sim = xb[core, q, :, 0:384], xb[core, q, :, 384:768]
        are, aim = cpl[q, :, 0:384], cpl[q, :, 384:768]
        cross_re = fold(sre * aim - sim * are)
        cross_im = -fold(sre * are + sim * aim)
        self_sq = fold(sre * sre + sim * sim)
        own_re, own_im = ratio(cross_re, self_sq), ratio(cross_im, self_sq)
        ore = aim - (own_re * sre - own_im * sim)
        oim = -are - (own_re * sim + own_im * sre)
        left = fold(ore * ore + oim * oim)
        for i, value in enumerate((cross_re, cross_im, self_sq, left)):
            stat[q, i : i + 1, :] = jnp.broadcast_to(value, (1, LANES))

    def natural(piece):
        out = []
        for plane in range(2):
            cols = [slice((plane * 3 + i) * LANES, (plane * 3 + i + 1) * LANES) for i in range(3)]
            parts = [flat4(*(piece(s, c) for c in cols)) for s in range(4)]
            for i in range(4):
                out.append(jnp.concatenate([p[i] for p in parts], axis=1))
        return out

    def lay(target, q, quad, values):
        for i, value in enumerate(values):
            row = (i // 4) * B + 4 * q + i % 4
            for j in range(3):
                at = (3 * quad + j) * 256 + row
                target[pl.ds(at, 8, stride=2 * B), :] = value[:, j * LANES : j * LANES + LANES]

    def receive_state():
        for k in range(1, DEV):
            state_copy(k).wait_recv()

        @pl.loop(0, Q)
        def _(q):
            for quad in range(4):
                lay(s_nat, q, quad, natural(lambda s, c: srecv[4 * quad + s, q, :, c]))

    def kinetic(elements):
        high = functools.partial(
            lax.dot_general, precision=lax.Precision.HIGHEST, preferred_element_type=F32
        )
        same = (((1,), (1,)), ((), ()))
        flip = (((1,), (0,)), ((), ()))
        for e in elements:
            here = [slice(256 * x, 256 * x + 256) for x in (e - 1, e, e + 1)]
            value = high(s_nat[here[1], :], diag_v[e], same)
            if e > 0:
                value = value + high(s_nat[here[0], :], link_v[e - 1], same)
            if e < 11:
                value = value + high(s_nat[here[2], :], link_v[e], flip)
            k_nat[here[1], :] = value

    def send_kinetic():
        @pl.loop(0, Q)
        def _(q):
            for plane in range(2):
                for quad in range(4):
                    rows = [
                        jnp.concatenate(
                            [
                                k_nat[
                                    pl.ds((3 * quad + j) * 256 + plane * B + 4 * q + i, 8, stride=2 * B),
                                    :,
                                ]
                                for j in range(3)
                            ],
                            axis=1,
                        )
                        for i in range(4)
                    ]
                    for s in range(4):
                        kout[4 * quad + s, q, :, plane * 384 : plane * 384 + 384] = jnp.concatenate(
                            [flat4(*(r[:, c * LANES : c * LANES + LANES] for c in range(3)))[s] for r in rows],
                            axis=1,
                        )

        for k in range(1, DEV):
            kinetic_copy(k).start()
        krecv[:, pl.ds(pl.multiple_of(8 * rad, 8), 8), :] = kout[rad]

    def receive_coupled(q):
        for k in range(1, DEV):
            coupled_copy(q, k).wait_recv()
        for quad in range(4):
            lay(a_nat, q, quad, natural(lambda s, c: crecv[q, 4 * quad + s, :, c]))

    for q in range(Q):
        sibx_copy(q).wait_recv()

    def chunk_round(n):
        return 2 * (n // (2 * T)) + lax.rem(n, 2), lax.rem(n, 2 * T) // 2

    @pl.loop(0, Q // 2)
    def _(pair):
        for t in range(T):

            @pl.loop(0, 2)
            def _(parity):
                q = 2 * pair + parity
                last = q - 2
                n = 2 * T * pair + 2 * t + parity

                @pl.when(n >= 3)
                def _():
                    ring_arrived(*chunk_round(n - 3))

                @pl.when(n >= 4)
                def _():
                    sib_arrived(*chunk_round(n - 4))

                ring_start(q, t)

                if t == 0:

                    @pl.when(q == 0)
                    def _():
                        build_coupling()

                if t == 1:

                    @pl.when(q == 0)
                    def _():
                        build(0)
                        build(1)

                    @pl.when(q == 1)
                    def _():
                        build_kern()

                if t < LAG and (T + t) % 2 and (T + t) // 2 < GROUPS - 1:

                    @pl.when(q > 1)
                    def _():
                        compute(last, (T + t) // 2)

                if t == 1:

                    @pl.when(q > 1)
                    def _():
                        compute(last, GROUPS - 1)
                        fold_orders(last)

                if t == 2:
                    compute(q, 0)
                if t > LAG and t % 2 and t // 2 < GROUPS - 1:
                    compute(q, t // 2)
                if t == 4:

                    @pl.when(q == 0)
                    def _():
                        build(2)
                        build(3)

                    @pl.when(q == 1)
                    def _():
                        receive_state()

                if t == 5:

                    @pl.when(q == 0)
                    def _():
                        loads[2].wait()
                        loads[3].wait()
                        kinetic(range(0, 6))

                    @pl.when(q == 1)
                    def _():
                        kinetic(range(6, 12))

                    @pl.when(q == 2)
                    def _():
                        for k in range(1, DEV):
                            kinetic_copy(k).wait_recv()

                    @pl.when(q > 1)
                    def _():
                        send_chunk(last)

                if t == 6:

                    @pl.when(q == 0)
                    def _():
                        send_kinetic()

                    @pl.when(q == 1)
                    def _():
                        for group in range(4, GROUPS):
                            build(group)

                if t == T - 1:

                    @pl.when(q > 1)
                    def _():
                        receive_coupled(last)

    steps = Q * T
    ring_arrived(*chunk_round(steps - 3))
    sib_arrived(*chunk_round(steps - 4))
    ring_arrived(*chunk_round(steps - 2))
    sib_arrived(*chunk_round(steps - 3))
    if T % 2:
        compute(Q - 2, GROUPS - 2)
        compute(Q - 1, GROUPS - 2)
    sib_arrived(*chunk_round(steps - 2))
    compute(Q - 2, GROUPS - 1)
    fold_orders(Q - 2)
    send_chunk(Q - 2)
    ring_arrived(*chunk_round(steps - 1))
    sib_arrived(*chunk_round(steps - 1))
    compute(Q - 1, GROUPS - 1)
    fold_orders(Q - 1)
    send_chunk(Q - 1)

    def merge(groups):
        rows = [[g[i] for g in groups] for i in range(4)]
        cre, cim, sq, rest = (functools.reduce(lambda x, y: x + y, r) for r in rows)
        pre, pim = ratio(cre, sq), ratio(cim, sq)
        for gre, gim, gsq, _ in groups:
            dre = pre - ratio(gre, gsq)
            dim = pim - ratio(gim, gsq)
            rest = rest + (dre * dre + dim * dim) * gsq
        return cre, cim, sq, rest, pre, pim

    def group_of(ref):
        return [ref[i : i + 1, :] for i in range(4)]

    def scalar_copy(hop, k):
        return pltpu.make_async_remote_copy(
            src_ref=part.at[hop],
            dst_ref=gath.at[hop, (me, rad)[hop]],
            send_sem=sc_send.at[hop, k],
            recv_sem=sc_recv.at[hop, k],
            device_id=(chan_peer, rad_peer)[hop](k),
            device_id_type=MESH,
        )

    def put(hop, merged):
        for i in range(4):
            part[hop, i : i + 1, :] = merged[i]
        for k in range(1, DEV):
            scalar_copy(hop, k).start()
        gath[hop, (me, rad)[hop]] = part[hop]

    def take_all(hop):
        for k in range(1, DEV):
            scalar_copy(hop, k).wait_recv()
        return merge([group_of(gath.at[hop, j]) for j in range(DEV)])

    part[...] = jnp.zeros(part.shape, F32)
    put(0, merge([group_of(stat.at[q]) for q in range(Q)]))
    put(1, take_all(0))
    receive_coupled(Q - 2)
    receive_coupled(Q - 1)
    _, _, _, rest, pre, pim = take_all(1)
    rms = jnp.sqrt(rest / (2.0 * C * B * R) + 1e-06)
    place = lax.broadcasted_iota(jnp.int32, (1, 3), 1)
    coef_ref[...] = jnp.where(
        place == 0, pre[:, 0:3], jnp.where(place == 1, pim[:, 0:3], rms[:, 0:3])
    )
    for tile in range(R // LANES):
        cols = slice(tile * LANES, tile * LANES + LANES)
        for channel in range(8):
            re = slice(tile * 256 + channel * 2 * B, tile * 256 + channel * 2 * B + B)
            im = slice(re.stop, re.stop + B)
            sre, sim, are, aim = s_nat[re, :], s_nat[im, :], a_nat[re, :], a_nat[im, :]
            at = channel * 2 * B
            out_ref[at : at + B, cols] = aim - (pre * sre - pim * sim)
            out_ref[at + B : at + 2 * B, cols] = -are - (pre * sim + pim * sre)

    for k in range(1, DEV):
        live_copy(k).wait_send()
        state_copy(k).wait_send()
        kinetic_copy(k).wait_send()
        scalar_copy(0, k).wait_send()
        scalar_copy(1, k).wait_send()

    @pl.loop(0, Q)
    def _(q):
        sibx_copy(q).wait_send()
        for t in range(T):
            for way in range(2):
                ring_copy(q, t, way).wait_send()
            sib_copy(q, t).wait_send()
        for k in range(1, DEV):
            coupled_copy(q, k).wait_send()


def per_device(
    state, coupling, fetch_group, live_slots, radius_one, radius_two, kinetic_diag, kinetic_link
):
    vmem = pl.BlockSpec(memory_space=pltpu.VMEM)
    smem = pl.BlockSpec(memory_space=pltpu.SMEM)
    hbm = pl.BlockSpec(memory_space=pl.ANY)
    dma = pltpu.SemaphoreType.DMA
    rows_n = -(-4 * T // 8) * 8
    out, coef, flag = pl.pallas_call(
        kernel,
        out_shape=(
            jax.ShapeDtypeStruct((8 * 2 * B, R), F32),
            jax.ShapeDtypeStruct((1, 3), F32),
            jax.ShapeDtypeStruct((1,), jnp.int32),
        ),
        in_specs=[hbm, hbm, smem, smem, smem, vmem, hbm, hbm],
        out_specs=(vmem, vmem, smem),
        scratch_shapes=[
            pltpu.VMEM((2 * B * PTS, 128), F32),
            pltpu.VMEM((4 * 16 * 4 * GS, GS), F32),
            pltpu.VMEM((12, 128, 128), F32),
            pltpu.VMEM((11, 128, 128), F32),
            pltpu.VMEM((2, Q, 128, CELLS), F32),
            pltpu.VMEM((Q, T * 4 * GS, CELLS), F32),
            pltpu.VMEM((2, Q, T, GS, CELLS), F32),
            pltpu.VMEM((512, 512), BF16),
            pltpu.VMEM((512, 512), BF16),
            pltpu.VMEM((GROUPS, 512, 256), BF16),
            pltpu.VMEM((GROUPS, 512, 256), BF16),
            pltpu.VMEM((Q, 4, 8, CELLS), F32),
            pltpu.VMEM((2, 512, CELLS), F32),
            pltpu.VMEM((Q, 128, CELLS), F32),
            pltpu.VMEM((DEV, Q, 8, CELLS), F32),
            pltpu.VMEM((Q, DEV, 8, CELLS), F32),
            pltpu.VMEM((R // LANES * 256, LANES), F32),
            pltpu.VMEM((R // LANES * 256, LANES), F32),
            pltpu.VMEM((R // LANES * 256, LANES), F32),
            pltpu.VMEM((DEV, Q, 8, CELLS), F32),
            pltpu.VMEM((Q, 128, CELLS), F32),
            pltpu.VMEM((Q, 8, LANES), F32),
            pltpu.VMEM((2, 8, LANES), F32),
            pltpu.VMEM((2, DEV, 8, LANES), F32),
            pltpu.VMEM((8, LANES), jnp.int32),
            pltpu.VMEM((DEV, 8, LANES), jnp.int32),
            pltpu.VMEM((rows_n, LANES), jnp.int32),
            pltpu.VMEM((rows_n, LANES), jnp.int32),
            pltpu.VMEM((rows_n, LANES), jnp.int32),
            pltpu.VMEM((8 + rows_n, LANES), jnp.int32),
            dma((4,)),
            dma((DEV,)),
            dma((DEV,)),
            dma((2, Q, T)),
            dma((2, Q, T)),
            dma((Q, T)),
            dma((Q, T)),
            dma((Q,)),
            dma((Q,)),
            dma((DEV,)),
            dma((DEV,)),
            dma((Q, DEV)),
            dma((Q, DEV)),
            dma((DEV,)),
            dma((DEV,)),
            dma((2, DEV)),
            dma((2, DEV)),
        ],
        compiler_params=pltpu.CompilerParams(
            collective_id=0, has_side_effects=True, vmem_limit_bytes=61 << 20
        ),
    )(
        state.transpose(1, 2, 3, 0).reshape(2 * B * PTS, 128),
        coupling.reshape(4 * 16 * 4 * GS, GS),
        fetch_group,
        live_slots,
        radius_one,
        radius_two.reshape(1, PTS),
        kinetic_diag,
        kinetic_link,
    )
    return lax.cond(
        flag[0] > 0,
        static_program,
        lambda *_: (out.reshape(8, 2, B, R), coef.reshape(3)),
        state,
        coupling,
        fetch_group,
        live_slots,
        radius_one,
        radius_two,
        kinetic_diag,
        kinetic_link,
    )


def solution(mesh):
    placed = (
        P("chan", None, None, "rad"),
        P("chan", None, None, None, None),
        P(),
        P("chan"),
        P(),
        P("rad"),
        P(),
        P(),
    )
    return jax.shard_map(
        per_device,
        mesh=mesh,
        in_specs=placed,
        out_specs=(P(("chan", "rad"), None, None, None), P()),
        check_vma=False,
    )
```
